32 devices in a mesh: groups: 2 (over x), span: 8 (over z, y), head: 2 (over core).
Axes of the slice: x: 2, y: 2, z: 4, core: 2. Of those that a mesh axis runs over, the one named last changes fastest.
Arguments:
- span_states: bfloat16 [2048, 4096], P(('groups', 'span'), 'head'), parts along dimension 0, may hold values from -1.5 to 1.5
- span_queries: bfloat16 [2048, 2048], P(('groups', 'span'), 'head'), parts along dimension 0, may hold values from -1000 to 1000
- span_memory: bfloat16 [2048, 2, 896], P(('groups', 'span'), None, 'head'), parts along dimension 0, may hold values from -1000 to 1000
- passages: bfloat16 [16384, 896], P(('groups', 'span')), parts along dimension 0, may hold values from -1.5 to 1.5
- neighbours: int32 [32, 2], P(('groups', 'span')), parts along dimension 0, may hold values from 0 to 63, as said below
- enc_query_w: bfloat16 [896, 896], P(None, 'head'), may hold values from -0.1875 to 0.1875
- enc_out_w: bfloat16 [896, 896], P(None, 'head'), may hold values from -0.1875 to 0.1875
- kv_weight: bfloat16 [896, 2, 2048], P(None, None, ('head', 'span')), may hold values from -0.1875 to 0.1875
- out_weight: bfloat16 [2048, 4096], P('head', 'span'), may hold values from -0.125 to 0.125
Outputs:
- mixed_states: bfloat16 [2048, 4096], P(('groups', 'span'), 'head'), parts along dimension 0
The draws below stay inside these ranges and needn't reach their ends.
There are 2 independent parts, one for each index of `groups`. The reference program is written for one: setup_inputs(seed, part) draws one part's arguments, and reference() takes and returns one part's arrays. A program takes and returns all parts, laid end to end along the dimension named above; an argument that names none is the same for every part. Nothing has to cross between parts.
Inputs may be any that keep to these rules, and one draw needn't show every extreme that they name: `neighbours`: passage p belongs to index p // 8 of the span axis. Among the spans of one index of the span axis, all 4 passages listed belong to distinct indices.
All inputs are finite; a program needn't handle non-finite values.
Results may differ from the reference program's by a relative error of at most 0.025.
Values may be sent and summed in bfloat16 or wider, within the bound.
A program may use at most 64 MiB of HBM per device.

```python
import math
import jax
import jax.numpy as jnp
from jax import lax

D = 4096
HEADS = 16
HD = 128
E = 896
EHD = 64
CT = 64
PT = 128
NB = 2
PS_DEV = 8
CH_DEV = 2
SPANS = 16
PASSAGES = 64
N_HEAD = 2


def draw_neighbours(key, part):
    device_count = SPANS // CH_DEV

    def per_device(device_key):
        key_order, key_local = jax.random.split(device_key, 2)
        shuffled = jax.random.permutation(key_order, device_count)
        owners = shuffled[:CH_DEV * NB].reshape(CH_DEV, NB)
        local_ids = jax.random.randint(key_local, (CH_DEV, NB), 0, PS_DEV)
        return (owners * PS_DEV + local_ids).astype(jnp.int32)
    device_keys = jax.random.split(jax.random.fold_in(key, 11), device_count)
    return jax.vmap(per_device)(device_keys).reshape(SPANS, NB)


def draw_span_queries(key, part):
    key_base = jax.random.fold_in(jax.random.fold_in(key, 21), 0)
    shape = (SPANS * CT, HEADS * HD)
    values = jnp.clip(jax.random.normal(key_base, shape, jnp.float32), -6.0, 6.0) * 2.0
    return jnp.clip(values, -1000.0, 1000.0).astype(jnp.bfloat16)


def draw_span_memory(key, part):
    key_base = jax.random.fold_in(jax.random.fold_in(key, 31), 0)
    shape = (SPANS * CT, 2, E)
    values = jnp.clip(jax.random.normal(key_base, shape, jnp.float32), -6.0, 6.0)
    return jnp.clip(values, -1000.0, 1000.0).astype(jnp.bfloat16)


def shard_levels(key, dims, cuts, least, largest):
    factor_of, own = 1.0, jax.random.fold_in(key, 6)
    for dim, parts in cuts:
        steps = jnp.exp(jax.random.uniform(jax.random.fold_in(own, dim), (parts,), jnp.float32, least / len(cuts), largest / len(cuts)))
        factor_of = factor_of * jnp.repeat(steps, dims[dim] // parts).reshape([-1 if axis == dim else 1 for axis in range(len(dims))])
    return factor_of


def normal_values(stream_key, shape, scale, reach, shards=(), held_as=jnp.bfloat16):
    gain = shard_levels(stream_key, shape, shards, -0.22, 0.18) if shards else 1.0
    values = jax.random.normal(stream_key, shape, jnp.float32) * scale * gain
    return jnp.minimum(jnp.maximum(values, -reach), reach).astype(held_as)


def setup_inputs(seed: int = 0, part: int = 0) -> dict:
    splits = jax.random.split(jax.random.key(seed), 10)
    part_splits = jax.random.split(jax.random.fold_in(splits[9], part), 10)
    span_states = normal_values(part_splits[0], (SPANS * CT, D), 0.25, 1.5, ((0, 8), (1, 2)))
    span_queries = draw_span_queries(jax.random.fold_in(jax.random.fold_in(splits[9], part), 71), part)
    span_memory = draw_span_memory(jax.random.fold_in(jax.random.fold_in(splits[9], part), 71), part)
    passages = normal_values(part_splits[3], (PASSAGES * PT, E), 0.25, 1.5, ((0, 8),))
    neighbours = draw_neighbours(jax.random.fold_in(jax.random.fold_in(splits[9], part), 71), part)
    enc_query_w = normal_values(splits[5], (E, E), E ** -0.5, 0.1875, ((1, 2),))
    enc_out_w = normal_values(splits[6], (E, E), E ** -0.5, 0.1875, ((1, 2),))
    kv_weight = normal_values(splits[7], (E, 2, HEADS * HD), E ** -0.5, 0.1875, ((2, 16),))
    out_weight = normal_values(splits[8], (HEADS * HD, D), (HEADS * HD) ** -0.5, 0.125, ((0, 2), (1, 8)))
    return dict(span_states=span_states, span_queries=span_queries, span_memory=span_memory, passages=passages, neighbours=neighbours, enc_query_w=enc_query_w, enc_out_w=enc_out_w, kv_weight=kv_weight, out_weight=out_weight)


def rms_rows(values):
    return values * lax.rsqrt(lax.optimization_barrier(jnp.mean(values * values, axis=-1, keepdims=True)) + 1e-06)

def reference(span_states, span_queries, span_memory, passages, neighbours, enc_query_w, enc_out_w, kv_weight, out_weight):
    blocks = passages.reshape(PASSAGES, PT, E)
    half_width = HEADS * HD // N_HEAD
    kv_flat = kv_weight.reshape(E, 2 * HEADS * HD)

    def one_span(span_items):
        chosen, queries, memory, states = span_items
        copies = blocks[chosen]
        flat_rows = copies.reshape(NB * PT, E).astype(jnp.float32)
        normed = rms_rows(flat_rows).astype(jnp.bfloat16)
        enc_query = jnp.dot(normed, enc_query_w, preferred_element_type=jnp.float32).astype(jnp.bfloat16)
        enc_query = enc_query.reshape(NB * PT, E // EHD, EHD)
        key_rows = memory[:, 0].reshape(CT, E // EHD, EHD)
        value_rows = memory[:, 1].reshape(CT, E // EHD, EHD)
        scores = jnp.einsum('qhd,khd->hqk', enc_query.astype(jnp.float32), key_rows.astype(jnp.float32)) / math.sqrt(EHD)
        weights = jax.nn.softmax(scores, axis=-1).astype(jnp.bfloat16)
        mixed_heads = jnp.einsum('hqk,khd->qhd', weights.astype(jnp.float32), value_rows.astype(jnp.float32))
        mixed_heads = mixed_heads.astype(jnp.bfloat16).reshape(NB * PT, E)
        branch = jnp.dot(mixed_heads, enc_out_w.T, preferred_element_type=jnp.float32)
        encoded = rms_rows(flat_rows + branch).astype(jnp.bfloat16)
        dec_kv = jnp.dot(encoded, kv_flat, preferred_element_type=jnp.float32).astype(jnp.bfloat16)
        dec_kv = dec_kv.reshape(NB * PT, 2, HEADS, HD)
        dec_query = queries.reshape(CT, HEADS, HD)
        dec_scores = jnp.einsum('qhd,khd->hqk', dec_query.astype(jnp.float32), dec_kv[:, 0].astype(jnp.float32)) / math.sqrt(HD)
        dec_weights = jax.nn.softmax(dec_scores, axis=-1).astype(jnp.bfloat16)
        attended = jnp.einsum('hqk,khd->qhd', dec_weights.astype(jnp.float32), dec_kv[:, 1].astype(jnp.float32))
        attended = attended.astype(jnp.bfloat16).reshape(CT, HEADS * HD)
        summed = states.astype(jnp.float32)
        for group_index in range(N_HEAD):
            lower = group_index * half_width
            partial_value = jnp.dot(attended[:, lower:lower + half_width], out_weight[lower:lower + half_width], preferred_element_type=jnp.float32)
            rounded = lax.optimization_barrier(partial_value.astype(jnp.bfloat16))
            summed = summed + rounded.astype(jnp.float32)
        return summed.astype(jnp.bfloat16)
    span_rows = lax.map(one_span, (neighbours, span_queries.reshape(SPANS, CT, HEADS * HD), span_memory.reshape(SPANS, CT, 2, E), span_states.reshape(SPANS, CT, D)))
    return span_rows.reshape(SPANS * CT, D)
```

```python
import functools
import math

import jax
import jax.numpy as jnp
from jax import lax
from jax.experimental import pallas as pl
from jax.experimental.pallas import tpu as pltpu
from jax.sharding import PartitionSpec as P

HD = 128
E = 896
EHD = 64
CT = 64
PT = 128
NB = 2
PS_DEV = 8
MESH = pl.DeviceIdType.MESH


epsilon = 1e-06


def rms_rows(values):
    return values * lax.rsqrt(jnp.mean(values * values, axis=-1, keepdims=True) + epsilon)


def softmax_rows(scores):
    top_score = jnp.max(scores, axis=-1, keepdims=True)
    raised = jnp.exp(scores - top_score)
    return raised / jnp.sum(raised, axis=-1, keepdims=True)


def ring_place(span, n):
    odd = span % 2
    return (1 - odd) * (span // 2) + odd * (n - 1 - span // 2)


def ring_span(place, n):
    back = place // (n // 2)
    return (1 - back) * (2 * place) + back * (2 * (n - 1 - place) + 1)


def remote(src, dst, send_sem, recv_sem, **where):
    return pltpu.make_async_remote_copy(
        src_ref=src, dst_ref=dst, send_sem=send_sem, recv_sem=recv_sem,
        device_id=where, device_id_type=MESH,
    )


class Ring:
    def __init__(self, n, own, slots, sems):
        me = lax.axis_index("span")
        self.n, self.own, self.slots, self.sems = n, own, slots, sems
        self.place = ring_place(me, n)
        self.targets = (ring_span((self.place + 1) % n, n), ring_span((self.place + n - 1) % n, n))
        self.steps = n // 2
        self.copies = {}

    def travels(self, t, side, k):
        return t < self.steps - 1 or k % 2 == side

    def block(self, t, side):
        n = self.n
        return ring_span((self.place + (n - t if side == 0 else t)) % n, n)

    def send(self, t, side, k):
        dst = self.slots(self.block(t, side))[k]
        copy = remote(
            self.own[k] if t == 0 else dst, dst,
            self.sems.at[0, side, t, k], self.sems.at[1, side, t, k], span=self.targets[side],
        )
        copy.start()
        self.copies[t, side, k] = copy

    def start(self):
        for k in range(len(self.own)):
            for side in range(2):
                if self.travels(0, side, k):
                    self.send(0, side, k)

    def advance(self, t, forward=None):
        for k in range(len(self.own)):
            for side in range(2):
                if self.travels(t, side, k):
                    self.copies[t, side, k].wait_recv()
                    if t + 1 < self.steps and self.travels(t + 1, side, k):
                        self.send(t + 1, side, k)
                    if forward is not None:
                        forward(t, side, k, self.block(t + 1, side))
        return [self.block(t + 1, side) for side in range(1 if t == self.steps - 1 else 2)]

    def finish(self):
        for copy in self.copies.values():
            copy.wait_send()


def weigh(scores, mask):
    scores = jnp.where(mask, scores, -jnp.inf)
    raised = jnp.exp(scores - jnp.max(scores, axis=-1, keepdims=True))
    return (raised * (1.0 / jnp.sum(raised, axis=-1, keepdims=True))).astype(jnp.bfloat16)


def same_span(shape, rows_each, lanes_each, spans):
    row = lax.broadcasted_iota(jnp.int32, shape, 0) // rows_each
    lane = (lax.broadcasted_iota(jnp.int32, shape, 1) // lanes_each) % spans
    return row == lane


def dot(a, b, dims=((1,), (0,))):
    return lax.dot_general(a, b, (dims, ((), ())), preferred_element_type=jnp.float32)


def greet_all(n):
    me = lax.axis_index("span")
    head = lax.axis_index("head")
    barrier = pltpu.get_barrier_semaphore()
    for d in range(n):
        for hop in range(2):
            if d or hop:
                pl.semaphore_signal(
                    barrier, inc=1,
                    device_id={"span": (me + d) % n, "head": (head + hop) % 2}, device_id_type=MESH,
                )
    return barrier, 2 * n - 1


def fetch_kernel(
    n, spans, nb_ref, pas_in, mem_ref, wq_ref, wo_ref, kv_ref, enc, kvg,
    pas_ref, nb_own, nbg, nbs, picks, got, swap, cop, mem, wq, wo, query, mixed,
    local_sem, nb_sem, pas_sem, swap_sem, w_sem, enc_sem, ring_sem, twin_sem,
):
    me = lax.axis_index("span")
    head = lax.axis_index("head")
    group = lax.axis_index("groups")
    other = 1 - head
    twin = group + 1 - 2 * (group % 2)
    part = group % 2
    half_rows = PT // 2
    half_e = wq_ref.shape[0]
    barrier, greeted = greet_all(n)
    pl.semaphore_signal(barrier, inc=1, device_id={"groups": twin}, device_id_type=MESH)
    loads = [pltpu.make_async_copy(pas_in, pas_ref, local_sem.at[7])]
    for copy in loads:
        copy.start()
    nb_own[...] = jnp.zeros_like(nb_own)
    nb_own[:spans, :NB] = nb_ref[...]
    pl.semaphore_wait(barrier, greeted + 1)

    nb_copies = []
    for d in range(1, n):
        copy = remote(nb_own, nbg.at[me], nb_sem.at[0, d], nb_sem.at[1, d], span=(me + d) % n)
        copy.start()
        nb_copies.append(copy)
    own_nb = pltpu.make_async_copy(nb_own, nbg.at[me], local_sem.at[0])
    own_nb.start()

    depth = kv_ref.shape[1]
    half, extra = depth // 2, depth // 28 * 3
    near, far = part, 1 - part

    def pieces(ref):
        return [
            ref.at[near, pl.ds(0, half)], ref.at[near, pl.ds(half, half)],
            ref.at[far, pl.ds(0, extra // 2)], ref.at[far, pl.ds(extra // 2, extra // 2)],
        ]

    ring = Ring(n, pieces(kv_ref), lambda block: pieces(kvg.at[block]), ring_sem)
    twins = [[] for _ in range(ring.steps)]

    def to_twin(t, side, k, block):
        if k < 2:
            lines = pl.ds(extra, half - extra) if k == 0 else pl.ds(half, half)
            piece = kvg.at[block, near, lines]
            copy = remote(piece, piece, twin_sem.at[0, side, t, k], twin_sem.at[1, side, t, k], groups=twin)
            copy.start()
            twins[t].append(copy)

    ring.start()
    mine = pl.ds(pl.multiple_of(head * half_e, half_e), half_e)
    w_copies, own_copies = [], []
    for i, (src, dst) in enumerate((
        (mem_ref.at[0], mem.at[0, mine]), (mem_ref.at[1], mem.at[1, mine]), (wq_ref, wq.at[mine]), (wo_ref, wo.at[mine]),
    )):
        w_copies.append(remote(src, dst, w_sem.at[0, i], w_sem.at[1, i], head=other))
        w_copies[-1].start()
        own_copies.append(pltpu.make_async_copy(src, dst, local_sem.at[3 + i]))
        own_copies[-1].start()
    own_copies.append(pltpu.make_async_copy(kv_ref, kvg.at[me], local_sem.at[1]))
    own_copies[-1].start()
    own_nb.wait()
    loads[0].wait()
    for copy in nb_copies:
        copy.wait()
    to_scalar = pltpu.make_async_copy(nbg, nbs, local_sem.at[2])
    to_scalar.start()
    to_scalar.wait()

    def pick(requester):
        index = jnp.int32(0)
        for e in range(spans * NB):
            wanted = nbs[requester, e // NB, e % NB]
            index = index + jnp.where(wanted // PS_DEV == me, wanted % PS_DEV, 0)
        return pas_ref[index, head]

    pas_copies = []
    picks[1] = pick((me + 1) % n)
    for d in range(1, n):
        if d + 1 < n:
            picks[d + 1] = pick((me + d + 1) % n)
        else:
            got[me] = pick(me)
        copy = remote(picks.at[d], got.at[me], pas_sem.at[0, d], pas_sem.at[1, d], span=(me + d) % n)
        copy.start()
        pas_copies.append(copy)

    arrivals = [ring.advance(0, to_twin)]
    for copy in pas_copies:
        copy.wait_recv()
    swaps = []
    for c in range(spans):
        swap[c] = got[nbs[me, c, other] // PS_DEV]
    for c in range(spans):
        spot = cop.at[pl.ds(pl.multiple_of(c * PT + head * half_rows, half_rows), half_rows)]
        copy = remote(swap.at[c], spot, swap_sem.at[0, c], swap_sem.at[1, c], head=other)
        copy.start()
        swaps.append(copy)
        spot[...] = got[nbs[me, c, head] // PS_DEV]
    for copy in own_copies:
        copy.wait()
    for copy in w_copies:
        copy.wait()
    for copy in swaps:
        copy.wait()

    arrivals.append(ring.advance(1, to_twin))
    rows = cop.shape[0]
    tokens = mem.shape[2]
    width = cop.shape[1]
    values = cop[...].astype(jnp.float32)
    query[...] = dot(rms_rows(values).astype(jnp.bfloat16), wq[...], ((1,), (1,))).astype(jnp.bfloat16)
    mask = same_span((rows, tokens), PT, CT, spans)
    feature = lax.broadcasted_iota(jnp.int32, (2 * EHD, tokens), 0) // EHD
    for j in range(width // (2 * EHD)):
        lines = pl.ds(j * 2 * EHD, 2 * EHD)
        total = None
        for e in range(2):
            keys = jnp.where(feature == e, mem[0, lines], jnp.bfloat16(0))
            vals = jnp.where(feature == e, mem[1, lines], jnp.bfloat16(0))
            scores = dot(query[:, lines], keys) * (1.0 / math.sqrt(EHD))
            term = dot(weigh(scores, mask), vals, ((1,), (1,)))
            total = term if e == 0 else total + term
        mixed[:, lines] = total.astype(jnp.bfloat16)
    branch = dot(mixed[...], wo[...])
    enc[head] = rms_rows(cop[...].astype(jnp.float32) + branch).astype(jnp.bfloat16)
    enc_copy = remote(enc.at[head], enc.at[head], enc_sem.at[0], enc_sem.at[1], head=other)
    enc_copy.start()
    if ring.steps > 2:
        arrivals.append(ring.advance(2, to_twin))
    enc_copy.wait_recv()

    for t in range(ring.steps):
        while len(arrivals) < min(t + 3, ring.steps):
            arrivals.append(ring.advance(len(arrivals), to_twin))
        for copy in twins[t]:
            copy.wait_recv()
    enc_copy.wait_send()
    for copy in pas_copies + [copy for pair in twins for copy in pair]:
        copy.wait_send()
    ring.finish()


def line_order(z, length, j):
    far_half = z // max(1, length // 2)
    short = (1 - far_half) * z + far_half * (length - 1 - z)
    way = 1 - 2 * far_half
    both = (2 * short - j + 2 * length) // (2 * length)
    turn = 1 - 2 * (j % 2)
    source = z + both * turn * way * ((j + 1) // 2) + (1 - both) * way * (j - short)
    travel = -(both * turn * way + (1 - both) * way)
    return source, travel


def span_kernel(
    n, spans, nb_ref, pas_in, mem_ref, wq_ref, wo_ref, kv_ref, ask_in, w_in, states_in, out_ref,
    enc, kvg, att_ref, w_all, states_ref, gathered, partial, crossed, summed, back,
    pas_ref, ask_ref, nb_own, nbg, nbs, picks, got, swap, cop, mem, wq, wo, query, mixed,
    local_sem, nb_sem, pas_sem, swap_sem, w_sem, enc_sem, kvz_sem, kvy_sem, kvx_sem,
    wy_sem, wx_sem, att_sem, fwd_sem, cross_sem, send_sem, back_sem,
):
    me = lax.axis_index("span")
    head = lax.axis_index("head")
    group = lax.axis_index("groups")
    other = 1 - head
    twin = group + 1 - 2 * (group % 2)
    plane = group % 2
    length = n // 2
    z, y = me // 2, me % 2
    half_rows = PT // 2
    half_e = wq_ref.shape[0]
    pending = []

    def go(copy, cond=None):
        if cond is None:
            copy.start()
        else:
            pl.when(cond)(copy.start)
        pending.append((copy, cond))

    barrier, greeted = greet_all(n)
    pl.semaphore_signal(barrier, inc=1, device_id={"groups": twin}, device_id_type=MESH)
    loads = [
        pltpu.make_async_copy(pas_in, pas_ref, local_sem.at[7]),
        pltpu.make_async_copy(ask_in, ask_ref, local_sem.at[8]),
        pltpu.make_async_copy(w_in, w_all.at[y], local_sem.at[9]),
        pltpu.make_async_copy(states_in, states_ref, local_sem.at[10]),
    ]
    for copy in loads:
        copy.start()
    nb_own[...] = jnp.zeros_like(nb_own)
    nb_own[:spans, :NB] = nb_ref[...]
    pl.semaphore_wait(barrier, greeted + 1)

    for d in range(1, n):
        go(remote(nb_own, nbg.at[me], nb_sem.at[0, d], nb_sem.at[1, d], span=(me + d) % n))
    own_nb = pltpu.make_async_copy(nb_own, nbg.at[me], local_sem.at[0])
    own_nb.start()

    depth = kv_ref.shape[0]
    half, extra = depth // 2, depth // 56 * 3
    plane_lines = pl.ds(pl.multiple_of(plane * (half - extra), 16), half + extra)
    cross_lines = pl.ds(pl.multiple_of(plane * (half + extra), 16), half - extra)

    def along(source, travel, own):
        spot = kvg.at[2 * source + y, plane_lines]
        nxt = z + travel
        lane = (1 - travel) // 2
        copy = remote(
            kv_ref.at[plane_lines] if own else spot, spot, kvz_sem.at[0, source, lane], kvz_sem.at[1, source, lane],
            span=2 * ((nxt + length) % length) + y,
        )
        go(copy, (nxt >= 0) & (nxt < length))

    def to_pair(source, own):
        spot = kvg.at[2 * source + y, plane_lines]
        go(remote(
            kv_ref.at[plane_lines] if own else spot, spot, kvy_sem.at[0, source], kvy_sem.at[1, source],
            span=2 * z + 1 - y,
        ))

    def to_twin(block):
        spot = kvg.at[block, cross_lines]
        go(remote(spot, spot, kvx_sem.at[0, block], kvx_sem.at[1, block], groups=twin))

    def line_arrival(j):
        source, travel = line_order(z, length, j)
        lane = (1 - travel) // 2
        block = 2 * source + y
        spot = kvg.at[block, plane_lines]
        remote(spot, spot, kvz_sem.at[0, source, lane], kvz_sem.at[1, source, lane], span=2 * z + 1 - y).wait_recv()
        along(source, travel, False)
        to_pair(source, False)
        to_twin(block)

    def pair_arrival(j):
        source = z if j == 0 else line_order(z, length, j)[0]
        block = 2 * source + 1 - y
        spot = kvg.at[block, plane_lines]
        remote(spot, spot, kvy_sem.at[0, source], kvy_sem.at[1, source], span=2 * z + 1 - y).wait_recv()
        to_twin(block)

    def twin_arrival(block):
        lines = pl.ds(pl.multiple_of((1 - plane) * (half + extra), 16), half - extra)
        spot = kvg.at[block, lines]
        remote(spot, spot, kvx_sem.at[0, block], kvx_sem.at[1, block], groups=twin).wait_recv()

    for travel in (1, -1):
        along(z, travel, True)
    to_pair(z, True)

    mine = pl.ds(pl.multiple_of(head * half_e, half_e), half_e)
    w_copies, own_copies = [], []
    for i, (src, dst) in enumerate((
        (mem_ref.at[0], mem.at[0, mine]), (mem_ref.at[1], mem.at[1, mine]), (wq_ref, wq.at[mine]), (wo_ref, wo.at[mine]),
    )):
        w_copies.append(remote(src, dst, w_sem.at[0, i], w_sem.at[1, i], head=other))
        w_copies[-1].start()
        own_copies.append(pltpu.make_async_copy(src, dst, local_sem.at[3 + i]))
        own_copies[-1].start()
    own_copies.append(pltpu.make_async_copy(kv_ref, kvg.at[me], local_sem.at[1]))
    own_copies[-1].start()
    own_nb.wait()
    loads[0].wait()
    for d in range(1, n):
        pending[d - 1][0].wait_recv()
    to_scalar = pltpu.make_async_copy(nbg, nbs, local_sem.at[2])
    to_scalar.start()
    to_scalar.wait()

    def pick(requester):
        index = jnp.int32(0)
        for e in range(spans * NB):
            wanted = nbs[requester, e // NB, e % NB]
            index = index + jnp.where(wanted // PS_DEV == me, wanted % PS_DEV, 0)
        return pas_ref[index, head]

    pas_copies = []
    picks[1] = pick((me + 1) % n)
    for d in range(1, n):
        if d + 1 < n:
            picks[d + 1] = pick((me + d + 1) % n)
        else:
            got[me] = pick(me)
        copy = remote(picks.at[d], got.at[me], pas_sem.at[0, d], pas_sem.at[1, d], span=(me + d) % n)
        go(copy)
        pas_copies.append(copy)

    w_half = w_in.shape[0] // 2
    w_lines = pl.ds(pl.multiple_of(plane * w_half, 16), w_half)
    if length > 1:
        line_arrival(1)
    pair_arrival(0)
    w_pair = remote(w_in.at[w_lines], w_all.at[y, w_lines], wy_sem.at[0], wy_sem.at[1], span=2 * z + 1 - y)
    go(w_pair)
    for j in range(2, length):
        line_arrival(j)
        pair_arrival(j - 1)

    for copy in pas_copies:
        copy.wait_recv()
    swaps = []
    for c in range(spans):
        swap[c] = got[nbs[me, c, other] // PS_DEV]
    for c in range(spans):
        spot = cop.at[pl.ds(pl.multiple_of(c * PT + head * half_rows, half_rows), half_rows)]
        copy = remote(swap.at[c], spot, swap_sem.at[0, c], swap_sem.at[1, c], head=other)
        copy.start()
        swaps.append(copy)
        spot[...] = got[nbs[me, c, head] // PS_DEV]
    for copy in own_copies:
        copy.wait()
    for copy in w_copies:
        copy.wait()
    for copy in swaps:
        copy.wait()

    rows = cop.shape[0]
    tokens = mem.shape[2]
    width = cop.shape[1]
    values = cop[...].astype(jnp.float32)
    query[...] = dot(rms_rows(values).astype(jnp.bfloat16), wq[...], ((1,), (1,))).astype(jnp.bfloat16)
    mask = same_span((rows, tokens), PT, CT, spans)
    feature = lax.broadcasted_iota(jnp.int32, (2 * EHD, tokens), 0) // EHD
    for j in range(width // (2 * EHD)):
        lines = pl.ds(j * 2 * EHD, 2 * EHD)
        total = None
        for e in range(2):
            keys = jnp.where(feature == e, mem[0, lines], jnp.bfloat16(0))
            vals = jnp.where(feature == e, mem[1, lines], jnp.bfloat16(0))
            scores = dot(query[:, lines], keys) * (1.0 / math.sqrt(EHD))
            term = dot(weigh(scores, mask), vals, ((1,), (1,)))
            total = term if e == 0 else total + term
        mixed[:, lines] = total.astype(jnp.bfloat16)
    branch = dot(mixed[...], wo[...])
    enc[head] = rms_rows(cop[...].astype(jnp.float32) + branch).astype(jnp.bfloat16)
    enc_copy = remote(enc.at[head], enc.at[head], enc_sem.at[0], enc_sem.at[1], head=other)
    go(enc_copy)
    if length > 1:
        pair_arrival(length - 1)
    enc_copy.wait_recv()

    loads[1].wait()
    asks = ask_ref.shape[0]
    dec_mask = same_span((asks, NB * rows), CT, PT, spans)

    def send_attended(block):
        for travel in (1, -1):
            nxt = z + travel
            lane = (1 - travel) // 2
            copy = remote(
                att_ref.at[block], gathered.at[z, block], att_sem.at[0, lane, block], att_sem.at[1, lane, z],
                span=2 * ((nxt + length) % length) + y,
            )
            go(copy, (nxt >= 0) & (nxt < length))

    def attend(block):
        flat = enc[...].reshape(NB * rows, width)
        both = dot(flat, kvg[block]).astype(jnp.bfloat16)
        spot = pl.ds(pl.multiple_of(block * HD, HD), HD)
        scores = dot(ask_ref[:, spot], both[:, :HD], ((1,), (1,))) * (1.0 / math.sqrt(HD))
        att_ref[block] = dot(weigh(scores, dec_mask), both[:, HD:]).astype(jnp.bfloat16)
        send_attended(block)

    attend(me)
    w_back = pl.ds(pl.multiple_of((1 - plane) * w_half, 16), w_half)
    w_pair.wait_recv()
    crossing_w = w_all.at[1 - y, w_lines]
    go(remote(crossing_w, crossing_w, wx_sem.at[0], wx_sem.at[1], groups=twin))
    for j in range(length):
        if j:
            block = 2 * line_order(z, length, j)[0] + y
            twin_arrival(block)
            attend(block)
        block = 2 * (line_order(z, length, j)[0] if j else z) + 1 - y
        twin_arrival(block)
        attend(block)

    owner_head = z // (length // 2)
    column = z % (length // 2)
    out_rows = asks // 2
    w_width = w_in.shape[1]
    crossings, returns = [], []
    loads[2].wait()
    loads[3].wait()
    remote(
        w_all.at[1 - y, w_back], w_all.at[1 - y, w_back], wx_sem.at[0], wx_sem.at[1], groups=twin,
    ).wait_recv()

    def project(place, rows_ref):
        i = len(crossings)
        whole = jnp.concatenate([rows_ref[m] for m in range(n)], axis=1)
        for k in range(2):
            value = dot(whole, w_all[k]).astype(jnp.bfloat16)
            lanes = pl.ds(k * w_width, w_width)
            partial[i, 0, :, lanes] = value[:out_rows]
            partial[i, 1, :, lanes] = value[out_rows:]
        copy = remote(partial.at[i, other], crossed.at[i], cross_sem.at[0, i], cross_sem.at[1, i], head=other)
        go(copy)
        crossings.append((copy, place))

    def give_back():
        i = len(returns)
        copy, place = crossings[i]
        copy.wait_recv()
        total = partial[i, head].astype(jnp.float32) + crossed[i].astype(jnp.float32)
        summed[i] = total.astype(jnp.bfloat16)
        copy = remote(
            summed.at[i], back.at[column, head], send_sem.at[i], back_sem.at[column, head],
            span=2 * place + y, head=owner_head,
        )
        if i == 0:
            @pl.when(head == owner_head)
            def _():
                back[column, head] = summed[i]

            go(copy, head != owner_head)
        else:
            go(copy)
        returns.append(copy)

    project(z, att_ref)
    for j in range(1, length):
        source, travel = line_order(z, length, j)
        lane = (1 - travel) // 2
        slot = gathered.at[source]
        nxt = z + travel
        remote(slot, slot, att_sem.at[0, lane, 0], att_sem.at[1, lane, source], span=2 * z + 1 - y).wait_recv()
        copy = remote(
            slot, slot, fwd_sem.at[j], att_sem.at[1, lane, source], span=2 * ((nxt + length) % length) + y,
        )
        go(copy, (nxt >= 0) & (nxt < length))
        project(source, slot)
        give_back()
    give_back()

    wide = 2 * w_width
    for j in range(length // 2):
        for source in range(2):
            local = (head * (length // 2) + j == z) & (head == source)

            @pl.when(jnp.logical_not(local))
            def _():
                remote(
                    summed.at[0], back.at[j, source], send_sem.at[0], back_sem.at[j, source], head=other,
                ).wait_recv()

            lanes = pl.ds(j * wide, wide)
            lines = pl.ds(source * out_rows, out_rows)
            out_ref[lines, lanes] = (
                states_ref[lines, lanes].astype(jnp.float32) + back[j, source].astype(jnp.float32)
            ).astype(jnp.bfloat16)
    for copy, cond in pending:
        if cond is None:
            copy.wait_send()
        else:
            pl.when(cond)(copy.wait_send)


def out_kernel(n, *refs):
    barrier, greeted = greet_all(n)
    pl.semaphore_wait(barrier, greeted)
    out_stage(n, *refs)


def out_stage(
    n, att_ref, w_ref, states_ref, out_ref,
    gathered, part, crossed, summed, back, ring_sem, cross_sem, send_sem, back_sem,
):
    me = lax.axis_index("span")
    head = lax.axis_index("head")
    other = 1 - head
    half = n // 2
    owner_head = me // half
    column = me % half
    rows = att_ref.shape[0]
    half_rows = rows // 2
    width = w_ref.shape[1]

    def pieces(ref):
        return [ref.at[pl.ds(k * half_rows, half_rows)] for k in range(2)]

    ring = Ring(n, pieces(att_ref), lambda block: pieces(gathered.at[block]), ring_sem)
    ring.start()
    crossings, returns = [], []

    def project(block, rows_ref):
        i = len(crossings)
        value = jnp.dot(rows_ref[...], w_ref[...], preferred_element_type=jnp.float32)
        value = value.astype(jnp.bfloat16)
        part[i, 0] = value[:half_rows]
        part[i, 1] = value[half_rows:]
        copy = remote(part.at[i, other], crossed.at[i], cross_sem.at[0, i], cross_sem.at[1, i], head=other)
        crossings.append((copy, block))

    def send_across():
        crossings[-1][0].start()

    def give_back():
        i = len(returns)
        copy, block = crossings[i]
        copy.wait_recv()
        total = part[i, head].astype(jnp.float32) + crossed[i].astype(jnp.float32)
        summed[i] = total.astype(jnp.bfloat16)
        copy = remote(
            summed.at[i], back.at[column, head], send_sem.at[i], back_sem.at[column, head],
            span=block, head=owner_head,
        )
        if i == 0:
            @pl.when(head != owner_head)
            def _():
                copy.start()

            @pl.when(head == owner_head)
            def _():
                back[column, head] = summed[i]
        else:
            copy.start()
        returns.append(copy)

    project(me, att_ref)
    send_across()
    for t in range(ring.steps):
        for block in ring.advance(t):
            project(block, gathered.at[block])
            send_across()
            give_back()
    give_back()

    for j in range(half):
        for source in range(2):
            mine = (head * half + j == me) & (head == source)

            @pl.when(jnp.logical_not(mine))
            def _():
                remote(
                    summed.at[0], back.at[j, source], send_sem.at[0], back_sem.at[j, source], head=other,
                ).wait_recv()

            lanes = pl.ds(j * width, width)
            lines = pl.ds(source * half_rows, half_rows)
            out_ref[lines, lanes] = (
                states_ref[lines, lanes].astype(jnp.float32) + back[j, source].astype(jnp.float32)
            ).astype(jnp.bfloat16)
    ring.finish()
    for copy, _ in crossings:
        copy.wait_send()
    for i, copy in enumerate(returns):
        if i == 0:
            @pl.when(head != owner_head)
            def _():
                copy.wait_send()
        else:
            copy.wait_send()


def call(kernel, collective_id, out_shape, scratch_shapes, spaces, *operands):
    return pl.pallas_call(
        kernel,
        out_shape=out_shape,
        in_specs=[pl.BlockSpec(memory_space=space) for space in spaces],
        out_specs=[pl.BlockSpec(memory_space=pltpu.VMEM)] * len(out_shape),
        scratch_shapes=scratch_shapes,
        compiler_params=pltpu.CompilerParams(collective_id=collective_id, has_side_effects=True),
    )(*operands)


def decode(encoded, kv_all, span_queries, span_count):
    dec_kv = jnp.einsum(
        "re,nsec->rsnc", encoded.reshape(-1, E), kv_all, preferred_element_type=jnp.float32
    ).astype(jnp.bfloat16)
    head_count = span_queries.shape[1] // HD
    dec_kv = dec_kv.reshape(NB, span_count, PT, 2, head_count, HD)
    dec_query = span_queries.reshape(span_count, CT, head_count, HD)
    scores = jnp.einsum(
        "cqhd,ncphd->chqnp", dec_query, dec_kv[:, :, :, 0], preferred_element_type=jnp.float32
    ) / math.sqrt(HD)
    scores = scores.reshape(span_count, head_count, CT, NB * PT)
    weights = softmax_rows(scores).astype(jnp.bfloat16)
    weights = weights.reshape(span_count, head_count, CT, NB, PT)
    attended = jnp.einsum(
        "chqnp,ncphd->cqhd", weights, dec_kv[:, :, :, 1], preferred_element_type=jnp.float32
    )
    return attended.astype(jnp.bfloat16).reshape(span_count * CT, head_count * HD)


def body(
    span_states,
    span_queries,
    span_memory,
    passages,
    neighbours,
    enc_query_w,
    enc_out_w,
    kv_weight,
    out_weight,
):
    n = lax.axis_size("span")
    span_count = neighbours.shape[0]
    bf16 = jnp.bfloat16
    dma = pltpu.SemaphoreType.DMA
    half_rows = PT // 2
    memory = span_memory.transpose(1, 2, 0)
    rows, tokens = span_count * PT, span_memory.shape[0]
    sds = jax.ShapeDtypeStruct
    states, width = sds(span_states.shape, bf16), out_weight.shape[1]
    half = tokens // 2
    operands = (neighbours, passages.reshape(-1, 2, half_rows, E), memory, enc_query_w.T, enc_out_w.T)
    pas_scratch = [pltpu.VMEM((passages.shape[0] // PT, 2, half_rows, E), bf16)]
    scratch = [
        pltpu.VMEM((8, 128), jnp.int32),
        pltpu.VMEM((n, 8, 128), jnp.int32),
        pltpu.SMEM((n, 8, 128), jnp.int32),
        pltpu.VMEM((n, half_rows, E), bf16),
        pltpu.VMEM((n, half_rows, E), bf16),
        pltpu.VMEM((span_count, half_rows, E), bf16),
        pltpu.VMEM((rows, E), bf16),
        pltpu.VMEM((2, E, tokens), bf16),
        pltpu.VMEM((E, E), bf16),
        pltpu.VMEM((E, E), bf16),
        pltpu.VMEM((rows, E), bf16),
        pltpu.VMEM((rows, E), bf16),
        dma((11,)),
        dma((2, n)),
        dma((2, n)),
        dma((2, span_count)),
        dma((2, 4)),
        dma((2,)),
    ]
    if kv_weight.shape[2] == HD and n % 4 == 0:
        length = n // 2
        line_scratch = [
            pltpu.VMEM((NB, rows, E), bf16),
            pltpu.VMEM((n, E, 2 * HD), bf16),
            pltpu.VMEM((n, tokens, HD), bf16),
            pltpu.VMEM((2,) + out_weight.shape, bf16),
            pltpu.VMEM(span_states.shape, bf16),
            pltpu.VMEM((length, n, tokens, HD), bf16),
            pltpu.VMEM((length, 2, half, 2 * width), bf16),
            pltpu.VMEM((length, half, 2 * width), bf16),
            pltpu.VMEM((length, half, 2 * width), bf16),
            pltpu.VMEM((length // 2, 2, half, 2 * width), bf16),
        ]
        line_sems = [
            dma((2, length, 2)),
            dma((2, length)),
            dma((2, n)),
            dma((2,)),
            dma((2,)),
            dma((2, 2, n)),
            dma((length,)),
            dma((2, length)),
            dma((length,)),
            dma((length // 2, 2)),
        ]
        return call(
            functools.partial(span_kernel, n, span_count), 2, [states],
            line_scratch + pas_scratch + [pltpu.VMEM(span_queries.shape, bf16)] + scratch + line_sems,
            [pltpu.VMEM] + [pl.ANY] * 8,
            *operands, kv_weight.reshape(E, 2 * HD), span_queries, out_weight, span_states,
        )[0]
    kv = kv_weight.transpose(1, 0, 2)
    out_scratch = [
        pltpu.VMEM((n,) + span_queries.shape, bf16),
        pltpu.VMEM((n, 2, half, width), bf16),
        pltpu.VMEM((n, half, width), bf16),
        pltpu.VMEM((n, half, width), bf16),
        pltpu.VMEM((n // 2, 2, half, width), bf16),
        dma((2, 2, n // 2, 2)),
        dma((2, n)),
        dma((n,)),
        dma((n // 2, 2)),
    ]
    found = call(
        functools.partial(fetch_kernel, n, span_count), 0,
        [sds((NB, rows, E), bf16), sds((n,) + kv.shape, bf16)],
        pas_scratch + scratch + [dma((2, 2, n // 2, 4)), dma((2, 2, n // 2, 2))], [pltpu.VMEM] + [pl.ANY] * 5,
        *operands, kv,
    )
    attended = decode(found[0], found[1], span_queries, span_count)
    return call(
        functools.partial(out_kernel, n), 1, [states], out_scratch, [pltpu.VMEM] * 3,
        attended, out_weight, span_states,
    )[0]


def solution(mesh):
    placed = (
        P(("groups", "span"), "head"),
        P(("groups", "span"), "head"),
        P(("groups", "span"), None, "head"),
        P(("groups", "span"), None),
        P(("groups", "span"), None),
        P(None, "head"),
        P(None, "head"),
        P(None, None, ("head", "span")),
        P("head", "span"),
    )
    return jax.shard_map(
        body, mesh=mesh, in_specs=placed, out_specs=P(("groups", "span"), "head"), check_vma=False
    )
```

```python
import functools
import math

import jax
import jax.numpy as jnp
from jax import lax
from jax.experimental import pallas as pl
from jax.experimental.pallas import tpu as pltpu
from jax.sharding import PartitionSpec as P

HD = 128
E = 896
EHD = 64
CT = 64
PT = 128
NB = 2
PS_DEV = 8
MESH = pl.DeviceIdType.MESH


epsilon = 1e-06


def rms_rows(values):
    return values * lax.rsqrt(jnp.mean(values * values, axis=-1, keepdims=True) + epsilon)


def softmax_rows(scores):
    top_score = jnp.max(scores, axis=-1, keepdims=True)
    raised = jnp.exp(scores - top_score)
    return raised / jnp.sum(raised, axis=-1, keepdims=True)


def ring_place(span, n):
    odd = span % 2
    return (1 - odd) * (span // 2) + odd * (n - 1 - span // 2)


def ring_span(place, n):
    back = place // (n // 2)
    return (1 - back) * (2 * place) + back * (2 * (n - 1 - place) + 1)


def remote(src, dst, send_sem, recv_sem, **where):
    return pltpu.make_async_remote_copy(
        src_ref=src, dst_ref=dst, send_sem=send_sem, recv_sem=recv_sem,
        device_id=where, device_id_type=MESH,
    )


class Ring:
    def __init__(self, n, own, slots, sems):
        me = lax.axis_index("span")
        self.n, self.own, self.slots, self.sems = n, own, slots, sems
        self.place = ring_place(me, n)
        self.targets = (ring_span((self.place + 1) % n, n), ring_span((self.place + n - 1) % n, n))
        self.steps = n // 2
        self.copies = {}

    def travels(self, t, side, k):
        return t < self.steps - 1 or k % 2 == side

    def block(self, t, side):
        n = self.n
        return ring_span((self.place + (n - t if side == 0 else t)) % n, n)

    def send(self, t, side, k):
        dst = self.slots(self.block(t, side))[k]
        copy = remote(
            self.own[k] if t == 0 else dst, dst,
            self.sems.at[0, side, t, k], self.sems.at[1, side, t, k], span=self.targets[side],
        )
        copy.start()
        self.copies[t, side, k] = copy

    def start(self):
        for k in range(len(self.own)):
            for side in range(2):
                if self.travels(0, side, k):
                    self.send(0, side, k)

    def advance(self, t, forward=None):
        for k in range(len(self.own)):
            for side in range(2):
                if self.travels(t, side, k):
                    self.copies[t, side, k].wait_recv()
                    if t + 1 < self.steps and self.travels(t + 1, side, k):
                        self.send(t + 1, side, k)
                    if forward is not None:
                        forward(t, side, k, self.block(t + 1, side))
        return [self.block(t + 1, side) for side in range(1 if t == self.steps - 1 else 2)]

    def finish(self):
        for copy in self.copies.values():
            copy.wait_send()


def weigh(scores, mask):
    scores = jnp.where(mask, scores, -jnp.inf)
    raised = jnp.exp(scores - jnp.max(scores, axis=-1, keepdims=True))
    return (raised * (1.0 / jnp.sum(raised, axis=-1, keepdims=True))).astype(jnp.bfloat16)


def same_span(shape, rows_each, lanes_each, spans):
    row = lax.broadcasted_iota(jnp.int32, shape, 0) // rows_each
    lane = (lax.broadcasted_iota(jnp.int32, shape, 1) // lanes_each) % spans
    return row == lane


def dot(a, b, dims=((1,), (0,))):
    return lax.dot_general(a, b, (dims, ((), ())), preferred_element_type=jnp.float32)


def greet_all(n):
    me = lax.axis_index("span")
    head = lax.axis_index("head")
    barrier = pltpu.get_barrier_semaphore()
    for d in range(n):
        for hop in range(2):
            if d or hop:
                pl.semaphore_signal(
                    barrier, inc=1,
                    device_id={"span": (me + d) % n, "head": (head + hop) % 2}, device_id_type=MESH,
                )
    return barrier, 2 * n - 1


def fetch_kernel(
    n, spans, nb_ref, pas_in, mem_ref, wq_ref, wo_ref, kv_ref, enc, kvg,
    pas_ref, nb_own, nbg, nbs, picks, got, swap, cop, mem, wq, wo, query, mixed,
    local_sem, nb_sem, pas_sem, swap_sem, w_sem, enc_sem, ring_sem, twin_sem,
):
    me = lax.axis_index("span")
    head = lax.axis_index("head")
    group = lax.axis_index("groups")
    other = 1 - head
    twin = group + 1 - 2 * (group % 2)
    part = group % 2
    half_rows = PT // 2
    half_e = wq_ref.shape[0]
    barrier, greeted = greet_all(n)
    pl.semaphore_signal(barrier, inc=1, device_id={"groups": twin}, device_id_type=MESH)
    loads = [pltpu.make_async_copy(pas_in, pas_ref, local_sem.at[7])]
    for copy in loads:
        copy.start()
    nb_own[...] = jnp.zeros_like(nb_own)
    nb_own[:spans, :NB] = nb_ref[...]
    pl.semaphore_wait(barrier, greeted + 1)

    nb_copies = []
    for d in range(1, n):
        copy = remote(nb_own, nbg.at[me], nb_sem.at[0, d], nb_sem.at[1, d], span=(me + d) % n)
        copy.start()
        nb_copies.append(copy)
    own_nb = pltpu.make_async_copy(nb_own, nbg.at[me], local_sem.at[0])
    own_nb.start()

    depth = kv_ref.shape[1]
    half, extra = depth // 2, depth // 28 * 3
    near, far = part, 1 - part

    def pieces(ref):
        return [
            ref.at[near, pl.ds(0, half)], ref.at[near, pl.ds(half, half)],
            ref.at[far, pl.ds(0, extra // 2)], ref.at[far, pl.ds(extra // 2, extra // 2)],
        ]

    ring = Ring(n, pieces(kv_ref), lambda block: pieces(kvg.at[block]), ring_sem)
    twins = [[] for _ in range(ring.steps)]

    def to_twin(t, side, k, block):
        if k < 2:
            lines = pl.ds(extra, half - extra) if k == 0 else pl.ds(half, half)
            piece = kvg.at[block, near, lines]
            copy = remote(piece, piece, twin_sem.at[0, side, t, k], twin_sem.at[1, side, t, k], groups=twin)
            copy.start()
            twins[t].append(copy)

    ring.start()
    mine = pl.ds(pl.multiple_of(head * half_e, half_e), half_e)
    w_copies, own_copies = [], []
    for i, (src, dst) in enumerate((
        (mem_ref.at[0], mem.at[0, mine]), (mem_ref.at[1], mem.at[1, mine]), (wq_ref, wq.at[mine]), (wo_ref, wo.at[mine]),
    )):
        w_copies.append(remote(src, dst, w_sem.at[0, i], w_sem.at[1, i], head=other))
        w_copies[-1].start()
        own_copies.append(pltpu.make_async_copy(src, dst, local_sem.at[3 + i]))
        own_copies[-1].start()
    own_copies.append(pltpu.make_async_copy(kv_ref, kvg.at[me], local_sem.at[1]))
    own_copies[-1].start()
    own_nb.wait()
    loads[0].wait()
    for copy in nb_copies:
        copy.wait()
    to_scalar = pltpu.make_async_copy(nbg, nbs, local_sem.at[2])
    to_scalar.start()
    to_scalar.wait()

    def pick(requester):
        index = jnp.int32(0)
        for e in range(spans * NB):
            wanted = nbs[requester, e // NB, e % NB]
            index = index + jnp.where(wanted // PS_DEV == me, wanted % PS_DEV, 0)
        return pas_ref[index, head]

    pas_copies = []
    picks[1] = pick((me + 1) % n)
    for d in range(1, n):
        if d + 1 < n:
            picks[d + 1] = pick((me + d + 1) % n)
        else:
            got[me] = pick(me)
        copy = remote(picks.at[d], got.at[me], pas_sem.at[0, d], pas_sem.at[1, d], span=(me + d) % n)
        copy.start()
        pas_copies.append(copy)

    arrivals = [ring.advance(0, to_twin)]
    for copy in pas_copies:
        copy.wait_recv()
    swaps = []
    for c in range(spans):
        swap[c] = got[nbs[me, c, other] // PS_DEV]
    for c in range(spans):
        spot = cop.at[pl.ds(pl.multiple_of(c * PT + head * half_rows, half_rows), half_rows)]
        copy = remote(swap.at[c], spot, swap_sem.at[0, c], swap_sem.at[1, c], head=other)
        copy.start()
        swaps.append(copy)
        spot[...] = got[nbs[me, c, head] // PS_DEV]
    for copy in own_copies:
        copy.wait()
    for copy in w_copies:
        copy.wait()
    for copy in swaps:
        copy.wait()

    arrivals.append(ring.advance(1, to_twin))
    rows = cop.shape[0]
    tokens = mem.shape[2]
    width = cop.shape[1]
    values = cop[...].astype(jnp.float32)
    query[...] = dot(rms_rows(values).astype(jnp.bfloat16), wq[...], ((1,), (1,))).astype(jnp.bfloat16)
    mask = same_span((rows, tokens), PT, CT, spans)
    feature = lax.broadcasted_iota(jnp.int32, (2 * EHD, tokens), 0) // EHD
    for j in range(width // (2 * EHD)):
        lines = pl.ds(j * 2 * EHD, 2 * EHD)
        total = None
        for e in range(2):
            keys = jnp.where(feature == e, mem[0, lines], jnp.bfloat16(0))
            vals = jnp.where(feature == e, mem[1, lines], jnp.bfloat16(0))
            scores = dot(query[:, lines], keys) * (1.0 / math.sqrt(EHD))
            term = dot(weigh(scores, mask), vals, ((1,), (1,)))
            total = term if e == 0 else total + term
        mixed[:, lines] = total.astype(jnp.bfloat16)
    branch = dot(mixed[...], wo[...])
    enc[head] = rms_rows(cop[...].astype(jnp.float32) + branch).astype(jnp.bfloat16)
    enc_copy = remote(enc.at[head], enc.at[head], enc_sem.at[0], enc_sem.at[1], head=other)
    enc_copy.start()
    if ring.steps > 2:
        arrivals.append(ring.advance(2, to_twin))
    enc_copy.wait_recv()

    for t in range(ring.steps):
        while len(arrivals) < min(t + 3, ring.steps):
            arrivals.append(ring.advance(len(arrivals), to_twin))
        for copy in twins[t]:
            copy.wait_recv()
    enc_copy.wait_send()
    for copy in pas_copies + [copy for pair in twins for copy in pair]:
        copy.wait_send()
    ring.finish()


W_CUTS = 4
W_CROSS = 1
KV_EXTRA = 6
KV_CUTS = 2


def line_order(z, length, j):
    far_half = z // max(1, length // 2)
    short = (1 - far_half) * z + far_half * (length - 1 - z)
    way = 1 - 2 * far_half
    both = (2 * short - j + 2 * length) // (2 * length)
    turn = 1 - 2 * (j % 2)
    source = z + both * turn * way * ((j + 1) // 2) + (1 - both) * way * (j - short)
    travel = -(both * turn * way + (1 - both) * way)
    return source, travel


def span_kernel(
    n, spans, nb_ref, pas_in, mem_ref, wq_ref, wo_ref, kv_ref, ask_in, w_in, states_in, out_ref,
    enc, kvg, att_ref, w_all, states_ref, gathered, partial, crossed, summed, back,
    pas_ref, ask_ref, nb_own, nbg, nbs, picks, got, swap, cop, mem, wq, wo, query, mixed,
    local_sem, nb_sem, pas_sem, swap_sem, w_sem, enc_sem, kvz_sem, kvy_sem, kvx_sem,
    wy_sem, wx_sem, att_sem, cross_sem, send_sem, back_sem,
):
    me = lax.axis_index("span")
    head = lax.axis_index("head")
    group = lax.axis_index("groups")
    other = 1 - head
    twin = group + 1 - 2 * (group % 2)
    plane = group % 2
    length = n // 2
    z, y = me // 2, me % 2
    half_rows = PT // 2
    half_e = wq_ref.shape[0]
    pending = []

    def go(copy, cond=None, start=True, note=True):
        if start:
            if cond is None:
                copy.start()
            else:
                pl.when(cond)(copy.start)
        if note:
            pending.append((copy, cond))

    barrier, greeted = greet_all(n)
    pl.semaphore_signal(barrier, inc=1, device_id={"groups": twin}, device_id_type=MESH)
    loads = [
        pltpu.make_async_copy(pas_in, pas_ref, local_sem.at[7]),
        pltpu.make_async_copy(ask_in, ask_ref, local_sem.at[8]),
        pltpu.make_async_copy(w_in, w_all.at[y], local_sem.at[9]),
        pltpu.make_async_copy(states_in, states_ref, local_sem.at[10]),
    ]
    for copy in loads:
        copy.start()
    nb_own[...] = jnp.zeros_like(nb_own)
    nb_own[:spans, :NB] = nb_ref[...]
    pl.semaphore_wait(barrier, greeted + 1)

    for d in range(1, n):
        go(remote(nb_own, nbg.at[me], nb_sem.at[0, d], nb_sem.at[1, d], span=(me + d) % n))
    own_nb = pltpu.make_async_copy(nb_own, nbg.at[me], local_sem.at[0])
    own_nb.start()

    depth = kv_ref.shape[0]
    half, extra = depth // 2, depth // 56 * KV_EXTRA
    cut = (half + extra) // KV_CUTS
    parts = range(KV_CUTS)

    def from_edge(side, offset, size):
        return pl.ds(pl.multiple_of((1 - side) * offset + side * (depth - offset - size), 16), size)

    def plane_part(i):
        return from_edge(plane, i * cut, cut)

    def cross_part(side, i):
        start = min(i * cut, half - extra)
        return from_edge(side, start, min((i + 1) * cut, half - extra) - start)

    crossed_parts = [i for i in parts if i * cut < half - extra]

    def along(source, travel, i, own, **how):
        lines = plane_part(i)
        spot = kvg.at[2 * source + y, lines]
        nxt = z + travel
        lane = (1 - travel) // 2
        copy = remote(
            kv_ref.at[lines] if own else spot, spot, kvz_sem.at[0, source, lane, i], kvz_sem.at[1, source, lane, i],
            span=2 * ((nxt + length) % length) + y,
        )
        go(copy, (nxt >= 0) & (nxt < length), **how)

    def to_pair(source, i, own, **how):
        lines = plane_part(i)
        spot = kvg.at[2 * source + y, lines]
        go(remote(
            kv_ref.at[lines] if own else spot, spot, kvy_sem.at[0, source, i], kvy_sem.at[1, source, i],
            span=2 * z + 1 - y,
        ), **how)

    def to_twin(block, i, **how):
        if i in crossed_parts:
            spot = kvg.at[block, cross_part(plane, i)]
            go(remote(spot, spot, kvx_sem.at[0, block, i], kvx_sem.at[1, block, i], groups=twin), **how)

    def line_arrival(j, start=True, note=True):
        source, travel = line_order(z, length, j)
        lane = (1 - travel) // 2
        block = 2 * source + y
        for i in parts:
            spot = kvg.at[block, plane_part(i)]
            if start:
                remote(
                    spot, spot, kvz_sem.at[0, source, lane, i], kvz_sem.at[1, source, lane, i], span=2 * z + 1 - y,
                ).wait_recv()
            along(source, travel, i, False, start=start, note=note)
            to_pair(source, i, False, start=start, note=note)
            to_twin(block, i, start=start, note=note)

    def pair_arrival(j):
        source = z if j == 0 else line_order(z, length, j)[0]
        block = 2 * source + 1 - y
        for i in parts:
            spot = kvg.at[block, plane_part(i)]
            remote(spot, spot, kvy_sem.at[0, source, i], kvy_sem.at[1, source, i], span=2 * z + 1 - y).wait_recv()
            to_twin(block, i)

    def twin_arrival(block):
        for i in crossed_parts:
            spot = kvg.at[block, cross_part(1 - plane, i)]
            remote(spot, spot, kvx_sem.at[0, block, i], kvx_sem.at[1, block, i], groups=twin).wait_recv()

    for i in parts:
        for travel in (1, -1):
            along(z, travel, i, True)
        to_pair(z, i, True)

    mine = pl.ds(pl.multiple_of(head * half_e, half_e), half_e)
    w_copies, own_copies = [], []
    for i, (src, dst) in enumerate((
        (mem_ref.at[0], mem.at[0, mine]), (mem_ref.at[1], mem.at[1, mine]), (wq_ref, wq.at[mine]), (wo_ref, wo.at[mine]),
    )):
        w_copies.append(remote(src, dst, w_sem.at[0, i], w_sem.at[1, i], head=other))
        w_copies[-1].start()
        own_copies.append(pltpu.make_async_copy(src, dst, local_sem.at[3 + i]))
        own_copies[-1].start()
    own_copies.append(pltpu.make_async_copy(kv_ref, kvg.at[me], local_sem.at[1]))
    own_copies[-1].start()
    own_nb.wait()
    loads[0].wait()
    for d in range(1, n):
        pending[d - 1][0].wait_recv()
    to_scalar = pltpu.make_async_copy(nbg, nbs, local_sem.at[2])
    to_scalar.start()
    to_scalar.wait()

    def pick(requester):
        index = jnp.int32(0)
        for e in range(spans * NB):
            wanted = nbs[requester, e // NB, e % NB]
            index = index + jnp.where(wanted // PS_DEV == me, wanted % PS_DEV, 0)
        return pas_ref[index, head]

    pas_copies = []
    picks[1] = pick((me + 1) % n)
    for d in range(1, n):
        if d + 1 < n:
            picks[d + 1] = pick((me + d + 1) % n)
        else:
            got[me] = pick(me)
        copy = remote(picks.at[d], got.at[me], pas_sem.at[0, d], pas_sem.at[1, d], span=(me + d) % n)
        go(copy)
        pas_copies.append(copy)
    line_arrival(1)
    pair_arrival(0)
    inner = (z > 0) & (z < length - 1)
    pl.when(inner)(lambda: line_arrival(2, note=False))
    for copy in pas_copies:
        copy.wait_recv()
    swaps = []
    for c in range(spans):
        swap[c] = got[nbs[me, c, other] // PS_DEV]
    for c in range(spans):
        spot = cop.at[pl.ds(pl.multiple_of(c * PT + head * half_rows, half_rows), half_rows)]
        copy = remote(swap.at[c], spot, swap_sem.at[0, c], swap_sem.at[1, c], head=other)
        copy.start()
        swaps.append(copy)
        spot[...] = got[nbs[me, c, head] // PS_DEV]
    pl.when(jnp.logical_not(inner))(lambda: line_arrival(2, note=False))
    line_arrival(2, start=False)
    pair_arrival(1)
    for copy in own_copies:
        copy.wait()
    for copy in w_copies:
        copy.wait()
    for copy in swaps:
        copy.wait()
    rows = cop.shape[0]
    tokens = mem.shape[2]
    width = cop.shape[1]
    values = cop[...].astype(jnp.float32)
    query[...] = dot(rms_rows(values).astype(jnp.bfloat16), wq[...], ((1,), (1,))).astype(jnp.bfloat16)
    mask = same_span((rows, tokens), PT, CT, spans)
    feature = lax.broadcasted_iota(jnp.int32, (2 * EHD, tokens), 0) // EHD
    for j in range(width // (2 * EHD)):
        lines = pl.ds(j * 2 * EHD, 2 * EHD)
        total = None
        for e in range(2):
            keys = jnp.where(feature == e, mem[0, lines], jnp.bfloat16(0))
            vals = jnp.where(feature == e, mem[1, lines], jnp.bfloat16(0))
            scores = dot(query[:, lines], keys) * (1.0 / math.sqrt(EHD))
            term = dot(weigh(scores, mask), vals, ((1,), (1,)))
            total = term if e == 0 else total + term
        mixed[:, lines] = total.astype(jnp.bfloat16)
    branch = dot(mixed[...], wo[...])
    enc[head] = rms_rows(cop[...].astype(jnp.float32) + branch).astype(jnp.bfloat16)
    enc_copy = remote(enc.at[head], enc.at[head], enc_sem.at[0], enc_sem.at[1], head=other)
    go(enc_copy)
    for j in range(3, length):
        line_arrival(j)
        pair_arrival(j - 1)
    w_chunk = w_in.shape[0] // W_CUTS

    def w_part(side, i):
        lines = (1 - side) * i + side * (W_CUTS - 1 - i)
        return pl.ds(pl.multiple_of(lines * w_chunk, 16), w_chunk)

    w_pairs = []
    for i in range(W_CUTS - W_CROSS):
        lines = w_part(plane, i)
        w_pairs.append(remote(
            w_in.at[lines], w_all.at[y, lines], wy_sem.at[0, i], wy_sem.at[1, i], span=2 * z + 1 - y,
        ))
        go(w_pairs[-1])

    def w_forward(i):
        w_pairs[i].wait_recv()
        spot = w_all.at[1 - y, w_part(plane, i)]
        go(remote(spot, spot, wx_sem.at[0, i], wx_sem.at[1, i], groups=twin))

    def w_arrival(i):
        spot = w_all.at[1 - y, w_part(1 - plane, i)]
        remote(spot, spot, wx_sem.at[0, i], wx_sem.at[1, i], groups=twin).wait_recv()
    enc_copy.wait_recv()

    loads[1].wait()
    asks = ask_ref.shape[0]
    def send_attended(place):
        spot = pl.ds(2 * place, 2)
        for travel in (1, -1):
            nxt = z + travel
            lane = (1 - travel) // 2
            copy = remote(
                att_ref.at[spot], gathered.at[z, spot], att_sem.at[0, lane, z, place], att_sem.at[1, lane, z, place],
                span=2 * ((nxt + length) % length) + y,
            )
            go(copy, (nxt >= 0) & (nxt < length))

    dec_mask = same_span((asks, NB * rows), CT, PT, spans)

    def attend(block):
        flat = enc[...].reshape(NB * rows, width)
        keys = dot(flat, kvg[block, :, pl.ds(0, HD)]).astype(jnp.bfloat16)
        vals = dot(flat, kvg[block, :, pl.ds(HD, HD)]).astype(jnp.bfloat16)
        spot = pl.ds(pl.multiple_of(block * HD, HD), HD)
        scores = dot(ask_ref[:, spot], keys, ((1,), (1,))) * (1.0 / math.sqrt(HD))
        att_ref[block] = dot(weigh(scores, dec_mask), vals).astype(jnp.bfloat16)

    for j in range(length):
        source = line_order(z, length, j)[0] if j else z
        blocks = [2 * source + y, 2 * source + 1 - y]
        for block in blocks[0 if j else 1:]:
            twin_arrival(block)
        for block in blocks:
            attend(block)
        send_attended(source)
        if j == length - 1:
            for i in range(W_CROSS):
                w_forward(i)
        if j == 0:
            pair_arrival(length - 1)

    owner_head = z // (length // 2)
    column = z % (length // 2)
    out_rows = asks // 2
    w_width = w_in.shape[1]
    crossings, returns = [], []

    def attended_arrival(j):
        source, travel = line_order(z, length, j)
        lane = (1 - travel) // 2
        nxt = z + travel
        for i in range(length):
            place = line_order(source, length, i)[0] if i else source
            slot = gathered.at[source, pl.ds(2 * place, 2)]
            copy = remote(
                slot, slot, att_sem.at[0, lane, source, place], att_sem.at[1, lane, source, place],
                span=2 * ((nxt + length) % length) + y,
            )
            copy.wait_recv()
            go(copy, (nxt >= 0) & (nxt < length))
        return source, gathered.at[source]

    def project(slot, k, rows_ref, place):
        whole = jnp.concatenate([rows_ref[m] for m in range(n)], axis=1)
        value = dot(whole, w_all[k]).astype(jnp.bfloat16)
        partial[slot, k, 0] = value[:out_rows]
        partial[slot, k, 1] = value[out_rows:]
        copy = remote(
            partial.at[slot, k, other], crossed.at[slot, k], cross_sem.at[0, slot, k], cross_sem.at[1, slot, k], head=other,
        )
        go(copy)
        crossings.append((copy, slot, k, place))

    def give_back():
        copy, slot, k, place = crossings[len(returns)]
        copy.wait_recv()
        total = partial[slot, k, head].astype(jnp.float32) + crossed[slot, k].astype(jnp.float32)
        summed[slot, k] = total.astype(jnp.bfloat16)
        copy = remote(
            summed.at[slot, k], back.at[column, head, k], send_sem.at[slot, k], back_sem.at[column, head, k],
            span=2 * place + y, head=owner_head,
        )
        if slot == 0:
            @pl.when(head == owner_head)
            def _():
                back[column, head, k] = summed[slot, k]

            go(copy, head != owner_head)
        else:
            go(copy)
        returns.append(copy)

    loads[2].wait()
    loads[3].wait()
    arrived = [(att_ref, z)]

    def arrive(j):
        source, slot = attended_arrival(j)
        arrived.append((slot, source))

    def work(slot, k):
        project(slot, k, *arrived[slot])
        if len(crossings) > 1:
            give_back()
    work(0, y)
    for j in range(1, length - 1):
        arrive(j)
        work(j, y)
    for i in range(W_CROSS, W_CUTS - W_CROSS):
        w_pairs[i].wait_recv()
    for i in range(W_CROSS):
        w_arrival(i)
    for j in range(length - 1):
        work(j, 1 - y)
    arrive(length - 1)
    work(length - 1, y)
    work(length - 1, 1 - y)
    give_back()

    for j in range(length // 2):
        for source in range(2):
            for k in range(2):
                local = (head * (length // 2) + j == z) & (head == source)

                @pl.when(jnp.logical_not(local))
                def _():
                    remote(
                        summed.at[0, 0], back.at[j, source, k], send_sem.at[0, 0], back_sem.at[j, source, k], head=other,
                    ).wait_recv()

                lanes = pl.ds((2 * j + k) * w_width, w_width)
                lines = pl.ds(source * out_rows, out_rows)
                out_ref[lines, lanes] = (
                    states_ref[lines, lanes].astype(jnp.float32) + back[j, source, k].astype(jnp.float32)
                ).astype(jnp.bfloat16)
    for copy, cond in pending:
        if cond is None:
            copy.wait_send()
        else:
            pl.when(cond)(copy.wait_send)


def out_kernel(n, *refs):
    barrier, greeted = greet_all(n)
    pl.semaphore_wait(barrier, greeted)
    out_stage(n, *refs)


def out_stage(
    n, att_ref, w_ref, states_ref, out_ref,
    gathered, part, crossed, summed, back, ring_sem, cross_sem, send_sem, back_sem,
):
    me = lax.axis_index("span")
    head = lax.axis_index("head")
    other = 1 - head
    half = n // 2
    owner_head = me // half
    column = me % half
    rows = att_ref.shape[0]
    half_rows = rows // 2
    width = w_ref.shape[1]

    def pieces(ref):
        return [ref.at[pl.ds(k * half_rows, half_rows)] for k in range(2)]

    ring = Ring(n, pieces(att_ref), lambda block: pieces(gathered.at[block]), ring_sem)
    ring.start()
    crossings, returns = [], []

    def project(block, rows_ref):
        i = len(crossings)
        value = jnp.dot(rows_ref[...], w_ref[...], preferred_element_type=jnp.float32)
        value = value.astype(jnp.bfloat16)
        part[i, 0] = value[:half_rows]
        part[i, 1] = value[half_rows:]
        copy = remote(part.at[i, other], crossed.at[i], cross_sem.at[0, i], cross_sem.at[1, i], head=other)
        crossings.append((copy, block))

    def send_across():
        crossings[-1][0].start()

    def give_back():
        i = len(returns)
        copy, block = crossings[i]
        copy.wait_recv()
        total = part[i, head].astype(jnp.float32) + crossed[i].astype(jnp.float32)
        summed[i] = total.astype(jnp.bfloat16)
        copy = remote(
            summed.at[i], back.at[column, head], send_sem.at[i], back_sem.at[column, head],
            span=block, head=owner_head,
        )
        if i == 0:
            @pl.when(head != owner_head)
            def _():
                copy.start()

            @pl.when(head == owner_head)
            def _():
                back[column, head] = summed[i]
        else:
            copy.start()
        returns.append(copy)

    project(me, att_ref)
    send_across()
    for t in range(ring.steps):
        for block in ring.advance(t):
            project(block, gathered.at[block])
            send_across()
            give_back()
    give_back()

    for j in range(half):
        for source in range(2):
            mine = (head * half + j == me) & (head == source)

            @pl.when(jnp.logical_not(mine))
            def _():
                remote(
                    summed.at[0], back.at[j, source], send_sem.at[0], back_sem.at[j, source], head=other,
                ).wait_recv()

            lanes = pl.ds(j * width, width)
            lines = pl.ds(source * half_rows, half_rows)
            out_ref[lines, lanes] = (
                states_ref[lines, lanes].astype(jnp.float32) + back[j, source].astype(jnp.float32)
            ).astype(jnp.bfloat16)
    ring.finish()
    for copy, _ in crossings:
        copy.wait_send()
    for i, copy in enumerate(returns):
        if i == 0:
            @pl.when(head != owner_head)
            def _():
                copy.wait_send()
        else:
            copy.wait_send()


def call(kernel, collective_id, out_shape, scratch_shapes, spaces, *operands):
    return pl.pallas_call(
        kernel,
        out_shape=out_shape,
        in_specs=[pl.BlockSpec(memory_space=space) for space in spaces],
        out_specs=[pl.BlockSpec(memory_space=pltpu.VMEM)] * len(out_shape),
        scratch_shapes=scratch_shapes,
        compiler_params=pltpu.CompilerParams(collective_id=collective_id, has_side_effects=True),
    )(*operands)


def decode(encoded, kv_all, span_queries, span_count):
    dec_kv = jnp.einsum(
        "re,nsec->rsnc", encoded.reshape(-1, E), kv_all, preferred_element_type=jnp.float32
    ).astype(jnp.bfloat16)
    head_count = span_queries.shape[1] // HD
    dec_kv = dec_kv.reshape(NB, span_count, PT, 2, head_count, HD)
    dec_query = span_queries.reshape(span_count, CT, head_count, HD)
    scores = jnp.einsum(
        "cqhd,ncphd->chqnp", dec_query, dec_kv[:, :, :, 0], preferred_element_type=jnp.float32
    ) / math.sqrt(HD)
    scores = scores.reshape(span_count, head_count, CT, NB * PT)
    weights = softmax_rows(scores).astype(jnp.bfloat16)
    weights = weights.reshape(span_count, head_count, CT, NB, PT)
    attended = jnp.einsum(
        "chqnp,ncphd->cqhd", weights, dec_kv[:, :, :, 1], preferred_element_type=jnp.float32
    )
    return attended.astype(jnp.bfloat16).reshape(span_count * CT, head_count * HD)


def body(
    span_states,
    span_queries,
    span_memory,
    passages,
    neighbours,
    enc_query_w,
    enc_out_w,
    kv_weight,
    out_weight,
):
    n = lax.axis_size("span")
    span_count = neighbours.shape[0]
    bf16 = jnp.bfloat16
    dma = pltpu.SemaphoreType.DMA
    half_rows = PT // 2
    memory = span_memory.transpose(1, 2, 0)
    rows, tokens = span_count * PT, span_memory.shape[0]
    sds = jax.ShapeDtypeStruct
    states, width = sds(span_states.shape, bf16), out_weight.shape[1]
    half = tokens // 2
    operands = (neighbours, passages.reshape(-1, 2, half_rows, E), memory, enc_query_w.T, enc_out_w.T)
    pas_scratch = [pltpu.VMEM((passages.shape[0] // PT, 2, half_rows, E), bf16)]
    scratch = [
        pltpu.VMEM((8, 128), jnp.int32),
        pltpu.VMEM((n, 8, 128), jnp.int32),
        pltpu.SMEM((n, 8, 128), jnp.int32),
        pltpu.VMEM((n, half_rows, E), bf16),
        pltpu.VMEM((n, half_rows, E), bf16),
        pltpu.VMEM((span_count, half_rows, E), bf16),
        pltpu.VMEM((rows, E), bf16),
        pltpu.VMEM((2, E, tokens), bf16),
        pltpu.VMEM((E, E), bf16),
        pltpu.VMEM((E, E), bf16),
        pltpu.VMEM((rows, E), bf16),
        pltpu.VMEM((rows, E), bf16),
        dma((11,)),
        dma((2, n)),
        dma((2, n)),
        dma((2, span_count)),
        dma((2, 4)),
        dma((2,)),
    ]
    if kv_weight.shape[2] == HD and n % 4 == 0:
        length = n // 2
        line_scratch = [
            pltpu.VMEM((NB, rows, E), bf16),
            pltpu.VMEM((n, E, 2 * HD), bf16),
            pltpu.VMEM((n, tokens, HD), bf16),
            pltpu.VMEM((2,) + out_weight.shape, bf16),
            pltpu.VMEM(span_states.shape, bf16),
            pltpu.VMEM((length, n, tokens, HD), bf16),
            pltpu.VMEM((length, 2, 2, half, width), bf16),
            pltpu.VMEM((length, 2, half, width), bf16),
            pltpu.VMEM((length, 2, half, width), bf16),
            pltpu.VMEM((length // 2, 2, 2, half, width), bf16),
        ]
        line_sems = [
            dma((2, length, 2, KV_CUTS)),
            dma((2, length, KV_CUTS)),
            dma((2, n, KV_CUTS)),
            dma((2, W_CUTS)),
            dma((2, W_CUTS)),
            dma((2, 2, length, length)),
            dma((2, length, 2)),
            dma((length, 2)),
            dma((length // 2, 2, 2)),
        ]
        return call(
            functools.partial(span_kernel, n, span_count), 2, [states],
            line_scratch + pas_scratch + [pltpu.VMEM(span_queries.shape, bf16)] + scratch + line_sems,
            [pltpu.VMEM] + [pl.ANY] * 8,
            *operands, kv_weight.reshape(E, 2 * HD), span_queries, out_weight, span_states,
        )[0]
    kv = kv_weight.transpose(1, 0, 2)
    out_scratch = [
        pltpu.VMEM((n,) + span_queries.shape, bf16),
        pltpu.VMEM((n, 2, half, width), bf16),
        pltpu.VMEM((n, half, width), bf16),
        pltpu.VMEM((n, half, width), bf16),
        pltpu.VMEM((n // 2, 2, half, width), bf16),
        dma((2, 2, n // 2, 2)),
        dma((2, n)),
        dma((n,)),
        dma((n // 2, 2)),
    ]
    found = call(
        functools.partial(fetch_kernel, n, span_count), 0,
        [sds((NB, rows, E), bf16), sds((n,) + kv.shape, bf16)],
        pas_scratch + scratch + [dma((2, 2, n // 2, 4)), dma((2, 2, n // 2, 2))], [pltpu.VMEM] + [pl.ANY] * 5,
        *operands, kv,
    )
    attended = decode(found[0], found[1], span_queries, span_count)
    return call(
        functools.partial(out_kernel, n), 1, [states], out_scratch, [pltpu.VMEM] * 3,
        attended, out_weight, span_states,
    )[0]


def solution(mesh):
    placed = (
        P(("groups", "span"), "head"),
        P(("groups", "span"), "head"),
        P(("groups", "span"), None, "head"),
        P(("groups", "span"), None),
        P(("groups", "span"), None),
        P(None, "head"),
        P(None, "head"),
        P(None, None, ("head", "span")),
        P("head", "span"),
    )
    return jax.shard_map(
        body, mesh=mesh, in_specs=placed, out_specs=P(("groups", "span"), "head"), check_vma=False
    )
```

```python
import functools
import math

import jax
import jax.numpy as jnp
from jax import lax
from jax.experimental import pallas as pl
from jax.experimental.pallas import tpu as pltpu
from jax.sharding import PartitionSpec as P

HD = 128
E = 896
EHD = 64
CT = 64
PT = 128
NB = 2
PS_DEV = 8
MESH = pl.DeviceIdType.MESH


epsilon = 1e-06


def rms_rows(values):
    return values * lax.rsqrt(jnp.mean(values * values, axis=-1, keepdims=True) + epsilon)


def softmax_rows(scores):
    top_score = jnp.max(scores, axis=-1, keepdims=True)
    raised = jnp.exp(scores - top_score)
    return raised / jnp.sum(raised, axis=-1, keepdims=True)


def ring_place(span, n):
    odd = span % 2
    return (1 - odd) * (span // 2) + odd * (n - 1 - span // 2)


def ring_span(place, n):
    back = place // (n // 2)
    return (1 - back) * (2 * place) + back * (2 * (n - 1 - place) + 1)


def remote(src, dst, send_sem, recv_sem, **where):
    return pltpu.make_async_remote_copy(
        src_ref=src, dst_ref=dst, send_sem=send_sem, recv_sem=recv_sem,
        device_id=where, device_id_type=MESH,
    )


class Ring:
    def __init__(self, n, own, slots, sems):
        me = lax.axis_index("span")
        self.n, self.own, self.slots, self.sems = n, own, slots, sems
        self.place = ring_place(me, n)
        self.targets = (ring_span((self.place + 1) % n, n), ring_span((self.place + n - 1) % n, n))
        self.steps = n // 2
        self.copies = {}

    def travels(self, t, side, k):
        return t < self.steps - 1 or k % 2 == side

    def block(self, t, side):
        n = self.n
        return ring_span((self.place + (n - t if side == 0 else t)) % n, n)

    def send(self, t, side, k):
        dst = self.slots(self.block(t, side))[k]
        copy = remote(
            self.own[k] if t == 0 else dst, dst,
            self.sems.at[0, side, t, k], self.sems.at[1, side, t, k], span=self.targets[side],
        )
        copy.start()
        self.copies[t, side, k] = copy

    def start(self):
        for k in range(len(self.own)):
            for side in range(2):
                if self.travels(0, side, k):
                    self.send(0, side, k)

    def advance(self, t, forward=None):
        for k in range(len(self.own)):
            for side in range(2):
                if self.travels(t, side, k):
                    self.copies[t, side, k].wait_recv()
                    if t + 1 < self.steps and self.travels(t + 1, side, k):
                        self.send(t + 1, side, k)
                    if forward is not None:
                        forward(t, side, k, self.block(t + 1, side))
        return [self.block(t + 1, side) for side in range(1 if t == self.steps - 1 else 2)]

    def finish(self):
        for copy in self.copies.values():
            copy.wait_send()


def weigh(scores, mask):
    scores = jnp.where(mask, scores, -jnp.inf)
    raised = jnp.exp(scores - jnp.max(scores, axis=-1, keepdims=True))
    return (raised * (1.0 / jnp.sum(raised, axis=-1, keepdims=True))).astype(jnp.bfloat16)


def same_span(shape, rows_each, lanes_each, spans):
    row = lax.broadcasted_iota(jnp.int32, shape, 0) // rows_each
    lane = (lax.broadcasted_iota(jnp.int32, shape, 1) // lanes_each) % spans
    return row == lane


def dot(a, b, dims=((1,), (0,))):
    return lax.dot_general(a, b, (dims, ((), ())), preferred_element_type=jnp.float32)


def greet_all(n):
    me = lax.axis_index("span")
    head = lax.axis_index("head")
    barrier = pltpu.get_barrier_semaphore()
    for d in range(n):
        for hop in range(2):
            if d or hop:
                pl.semaphore_signal(
                    barrier, inc=1,
                    device_id={"span": (me + d) % n, "head": (head + hop) % 2}, device_id_type=MESH,
                )
    return barrier, 2 * n - 1


def fetch_kernel(
    n, spans, nb_ref, pas_in, mem_ref, wq_ref, wo_ref, kv_ref, enc, kvg,
    pas_ref, nb_own, nbg, nbs, picks, got, swap, cop, mem, wq, wo, query, mixed,
    local_sem, nb_sem, pas_sem, swap_sem, w_sem, enc_sem, ring_sem, twin_sem,
):
    me = lax.axis_index("span")
    head = lax.axis_index("head")
    group = lax.axis_index("groups")
    other = 1 - head
    twin = group + 1 - 2 * (group % 2)
    part = group % 2
    half_rows = PT // 2
    half_e = wq_ref.shape[0]
    barrier, greeted = greet_all(n)
    pl.semaphore_signal(barrier, inc=1, device_id={"groups": twin}, device_id_type=MESH)
    loads = [pltpu.make_async_copy(pas_in, pas_ref, local_sem.at[7])]
    for copy in loads:
        copy.start()
    nb_own[...] = jnp.zeros_like(nb_own)
    nb_own[:spans, :NB] = nb_ref[...]
    pl.semaphore_wait(barrier, greeted + 1)

    nb_copies = []
    for d in range(1, n):
        copy = remote(nb_own, nbg.at[me], nb_sem.at[0, d], nb_sem.at[1, d], span=(me + d) % n)
        copy.start()
        nb_copies.append(copy)
    own_nb = pltpu.make_async_copy(nb_own, nbg.at[me], local_sem.at[0])
    own_nb.start()

    depth = kv_ref.shape[1]
    half, extra = depth // 2, depth // 28 * 3
    near, far = part, 1 - part

    def pieces(ref):
        return [
            ref.at[near, pl.ds(0, half)], ref.at[near, pl.ds(half, half)],
            ref.at[far, pl.ds(0, extra // 2)], ref.at[far, pl.ds(extra // 2, extra // 2)],
        ]

    ring = Ring(n, pieces(kv_ref), lambda block: pieces(kvg.at[block]), ring_sem)
    twins = [[] for _ in range(ring.steps)]

    def to_twin(t, side, k, block):
        if k < 2:
            lines = pl.ds(extra, half - extra) if k == 0 else pl.ds(half, half)
            piece = kvg.at[block, near, lines]
            copy = remote(piece, piece, twin_sem.at[0, side, t, k], twin_sem.at[1, side, t, k], groups=twin)
            copy.start()
            twins[t].append(copy)

    ring.start()
    mine = pl.ds(pl.multiple_of(head * half_e, half_e), half_e)
    w_copies, own_copies = [], []
    for i, (src, dst) in enumerate((
        (mem_ref.at[0], mem.at[0, mine]), (mem_ref.at[1], mem.at[1, mine]), (wq_ref, wq.at[mine]), (wo_ref, wo.at[mine]),
    )):
        w_copies.append(remote(src, dst, w_sem.at[0, i], w_sem.at[1, i], head=other))
        w_copies[-1].start()
        own_copies.append(pltpu.make_async_copy(src, dst, local_sem.at[3 + i]))
        own_copies[-1].start()
    own_copies.append(pltpu.make_async_copy(kv_ref, kvg.at[me], local_sem.at[1]))
    own_copies[-1].start()
    own_nb.wait()
    loads[0].wait()
    for copy in nb_copies:
        copy.wait()
    to_scalar = pltpu.make_async_copy(nbg, nbs, local_sem.at[2])
    to_scalar.start()
    to_scalar.wait()

    def pick(requester):
        index = jnp.int32(0)
        for e in range(spans * NB):
            wanted = nbs[requester, e // NB, e % NB]
            index = index + jnp.where(wanted // PS_DEV == me, wanted % PS_DEV, 0)
        return pas_ref[index, head]

    pas_copies = []
    picks[1] = pick((me + 1) % n)
    for d in range(1, n):
        if d + 1 < n:
            picks[d + 1] = pick((me + d + 1) % n)
        else:
            got[me] = pick(me)
        copy = remote(picks.at[d], got.at[me], pas_sem.at[0, d], pas_sem.at[1, d], span=(me + d) % n)
        copy.start()
        pas_copies.append(copy)

    arrivals = [ring.advance(0, to_twin)]
    for copy in pas_copies:
        copy.wait_recv()
    swaps = []
    for c in range(spans):
        swap[c] = got[nbs[me, c, other] // PS_DEV]
    for c in range(spans):
        spot = cop.at[pl.ds(pl.multiple_of(c * PT + head * half_rows, half_rows), half_rows)]
        copy = remote(swap.at[c], spot, swap_sem.at[0, c], swap_sem.at[1, c], head=other)
        copy.start()
        swaps.append(copy)
        spot[...] = got[nbs[me, c, head] // PS_DEV]
    for copy in own_copies:
        copy.wait()
    for copy in w_copies:
        copy.wait()
    for copy in swaps:
        copy.wait()

    arrivals.append(ring.advance(1, to_twin))
    rows = cop.shape[0]
    tokens = mem.shape[2]
    width = cop.shape[1]
    values = cop[...].astype(jnp.float32)
    query[...] = dot(rms_rows(values).astype(jnp.bfloat16), wq[...], ((1,), (1,))).astype(jnp.bfloat16)
    mask = same_span((rows, tokens), PT, CT, spans)
    feature = lax.broadcasted_iota(jnp.int32, (2 * EHD, tokens), 0) // EHD
    for j in range(width // (2 * EHD)):
        lines = pl.ds(j * 2 * EHD, 2 * EHD)
        total = None
        for e in range(2):
            keys = jnp.where(feature == e, mem[0, lines], jnp.bfloat16(0))
            vals = jnp.where(feature == e, mem[1, lines], jnp.bfloat16(0))
            scores = dot(query[:, lines], keys) * (1.0 / math.sqrt(EHD))
            term = dot(weigh(scores, mask), vals, ((1,), (1,)))
            total = term if e == 0 else total + term
        mixed[:, lines] = total.astype(jnp.bfloat16)
    branch = dot(mixed[...], wo[...])
    enc[head] = rms_rows(cop[...].astype(jnp.float32) + branch).astype(jnp.bfloat16)
    enc_copy = remote(enc.at[head], enc.at[head], enc_sem.at[0], enc_sem.at[1], head=other)
    enc_copy.start()
    if ring.steps > 2:
        arrivals.append(ring.advance(2, to_twin))
    enc_copy.wait_recv()

    for t in range(ring.steps):
        while len(arrivals) < min(t + 3, ring.steps):
            arrivals.append(ring.advance(len(arrivals), to_twin))
        for copy in twins[t]:
            copy.wait_recv()
    enc_copy.wait_send()
    for copy in pas_copies + [copy for pair in twins for copy in pair]:
        copy.wait_send()
    ring.finish()


W_CUTS = 4
W_CROSS = 1
KV_EXTRA = 6
KV_CUTS = 2


def line_order(z, length, j, first=-1):
    far_half = z // max(1, length // 2)
    short = (1 - far_half) * z + far_half * (length - 1 - z)
    way = 1 - 2 * far_half
    both = (2 * short - j + 2 * length) // (2 * length)
    turn = first * (2 * (j % 2) - 1)
    source = z + both * turn * way * ((j + 1) // 2) + (1 - both) * way * (j - short)
    travel = -(both * turn * way + (1 - both) * way)
    return source, travel


def span_kernel(
    n, spans, nb_ref, pas_in, mem_ref, wq_ref, wo_ref, kv_ref, ask_in, w_in, states_in, out_ref,
    enc, kvg, att_ref, w_all, states_ref, gathered, partial, crossed, summed, back,
    pas_ref, ask_ref, nb_own, nbg, nbs, picks, got, swap, cop, mem, wq, wo, query, mixed,
    local_sem, nb_sem, pas_sem, swap_sem, w_sem, enc_sem, kvz_sem, kvy_sem, kvx_sem,
    wy_sem, wx_sem, att_sem, cross_sem, send_sem, back_sem,
):
    me = lax.axis_index("span")
    head = lax.axis_index("head")
    group = lax.axis_index("groups")
    other = 1 - head
    twin = group + 1 - 2 * (group % 2)
    plane = group % 2
    length = n // 2
    z, y = me // 2, me % 2
    half_rows = PT // 2
    half_e = wq_ref.shape[0]
    pending = []

    def go(copy, cond=None, start=True, note=True):
        if start:
            if cond is None:
                copy.start()
            else:
                pl.when(cond)(copy.start)
        if note:
            pending.append((copy, cond))

    barrier, greeted = greet_all(n)
    pl.semaphore_signal(barrier, inc=1, device_id={"groups": twin}, device_id_type=MESH)
    loads = [
        pltpu.make_async_copy(pas_in, pas_ref, local_sem.at[7]),
        pltpu.make_async_copy(ask_in, ask_ref, local_sem.at[8]),
        pltpu.make_async_copy(w_in, w_all.at[y], local_sem.at[9]),
        pltpu.make_async_copy(states_in, states_ref, local_sem.at[10]),
    ]
    for copy in loads:
        copy.start()
    nb_own[...] = jnp.zeros_like(nb_own)
    nb_own[:spans, :NB] = nb_ref[...]
    pl.semaphore_wait(barrier, greeted + 1)

    for d in range(1, n):
        go(remote(nb_own, nbg.at[me], nb_sem.at[0, d], nb_sem.at[1, d], span=(me + d) % n))
    own_nb = pltpu.make_async_copy(nb_own, nbg.at[me], local_sem.at[0])
    own_nb.start()

    depth = kv_ref.shape[0]
    half, extra = depth // 2, depth // 56 * KV_EXTRA
    cut = (half + extra) // KV_CUTS
    parts = range(KV_CUTS)

    def from_edge(side, offset, size):
        return pl.ds(pl.multiple_of((1 - side) * offset + side * (depth - offset - size), 16), size)

    def plane_part(i):
        return from_edge(plane, i * cut, cut)

    def cross_part(side, i):
        start = min(i * cut, half - extra)
        return from_edge(side, start, min((i + 1) * cut, half - extra) - start)

    crossed_parts = [i for i in parts if i * cut < half - extra]

    def along(source, travel, i, own, **how):
        lines = plane_part(i)
        spot = kvg.at[2 * source + y, lines]
        nxt = z + travel
        lane = (1 - travel) // 2
        copy = remote(
            kv_ref.at[lines] if own else spot, spot, kvz_sem.at[0, source, lane, i], kvz_sem.at[1, source, lane, i],
            span=2 * ((nxt + length) % length) + y,
        )
        go(copy, (nxt >= 0) & (nxt < length), **how)

    def to_pair(source, i, own, **how):
        lines = plane_part(i)
        spot = kvg.at[2 * source + y, lines]
        go(remote(
            kv_ref.at[lines] if own else spot, spot, kvy_sem.at[0, source, i], kvy_sem.at[1, source, i],
            span=2 * z + 1 - y,
        ), **how)

    def to_twin(block, i, **how):
        if i in crossed_parts:
            spot = kvg.at[block, cross_part(plane, i)]
            go(remote(spot, spot, kvx_sem.at[0, block, i], kvx_sem.at[1, block, i], groups=twin), **how)

    def line_arrival(j, start=True, note=True):
        source, travel = line_order(z, length, j)
        lane = (1 - travel) // 2
        block = 2 * source + y
        for i in parts:
            spot = kvg.at[block, plane_part(i)]
            if start:
                remote(
                    spot, spot, kvz_sem.at[0, source, lane, i], kvz_sem.at[1, source, lane, i], span=2 * z + 1 - y,
                ).wait_recv()
            along(source, travel, i, False, start=start, note=note)
            to_pair(source, i, False, start=start, note=note)
            to_twin(block, i, start=start, note=note)

    def pair_arrival(j):
        source = z if j == 0 else line_order(z, length, j)[0]
        block = 2 * source + 1 - y
        for i in parts:
            spot = kvg.at[block, plane_part(i)]
            remote(spot, spot, kvy_sem.at[0, source, i], kvy_sem.at[1, source, i], span=2 * z + 1 - y).wait_recv()
            to_twin(block, i)

    def twin_arrival(block):
        for i in crossed_parts:
            spot = kvg.at[block, cross_part(1 - plane, i)]
            remote(spot, spot, kvx_sem.at[0, block, i], kvx_sem.at[1, block, i], groups=twin).wait_recv()

    for i in parts:
        for travel in (1, -1):
            along(z, travel, i, True)
        to_pair(z, i, True)

    mine = pl.ds(pl.multiple_of(head * half_e, half_e), half_e)
    w_copies, own_copies = [], []
    for i, (src, dst) in enumerate((
        (mem_ref.at[0], mem.at[0, mine]), (mem_ref.at[1], mem.at[1, mine]), (wq_ref, wq.at[mine]), (wo_ref, wo.at[mine]),
    )):
        w_copies.append(remote(src, dst, w_sem.at[0, i], w_sem.at[1, i], head=other))
        w_copies[-1].start()
        own_copies.append(pltpu.make_async_copy(src, dst, local_sem.at[3 + i]))
        own_copies[-1].start()
    own_copies.append(pltpu.make_async_copy(kv_ref, kvg.at[me], local_sem.at[1]))
    own_copies[-1].start()
    own_nb.wait()
    loads[0].wait()
    for d in range(1, n):
        pending[d - 1][0].wait_recv()
    to_scalar = pltpu.make_async_copy(nbg, nbs, local_sem.at[2])
    to_scalar.start()
    to_scalar.wait()

    def pick(requester):
        index = jnp.int32(0)
        for e in range(spans * NB):
            wanted = nbs[requester, e // NB, e % NB]
            index = index + jnp.where(wanted // PS_DEV == me, wanted % PS_DEV, 0)
        return pas_ref[index, head]

    pas_copies = []
    picks[1] = pick((me + 1) % n)
    for d in range(1, n):
        if d + 1 < n:
            picks[d + 1] = pick((me + d + 1) % n)
        else:
            got[me] = pick(me)
        copy = remote(picks.at[d], got.at[me], pas_sem.at[0, d], pas_sem.at[1, d], span=(me + d) % n)
        go(copy)
        pas_copies.append(copy)
    line_arrival(1)
    pair_arrival(0)
    inner = (z > 0) & (z < length - 1)
    pl.when(inner)(lambda: line_arrival(2, note=False))
    for copy in pas_copies:
        copy.wait_recv()
    swaps = []
    for c in range(spans):
        swap[c] = got[nbs[me, c, other] // PS_DEV]
    for c in range(spans):
        spot = cop.at[pl.ds(pl.multiple_of(c * PT + head * half_rows, half_rows), half_rows)]
        copy = remote(swap.at[c], spot, swap_sem.at[0, c], swap_sem.at[1, c], head=other)
        copy.start()
        swaps.append(copy)
        spot[...] = got[nbs[me, c, head] // PS_DEV]
    pl.when(jnp.logical_not(inner))(lambda: line_arrival(2, note=False))
    line_arrival(2, start=False)
    pair_arrival(1)
    for copy in own_copies:
        copy.wait()
    for copy in w_copies:
        copy.wait()
    for copy in swaps:
        copy.wait()
    rows = cop.shape[0]
    tokens = mem.shape[2]
    width = cop.shape[1]
    values = cop[...].astype(jnp.float32)
    query[...] = dot(rms_rows(values).astype(jnp.bfloat16), wq[...], ((1,), (1,))).astype(jnp.bfloat16)
    mask = same_span((rows, tokens), PT, CT, spans)
    feature = lax.broadcasted_iota(jnp.int32, (2 * EHD, tokens), 0) // EHD
    for j in range(width // (2 * EHD)):
        lines = pl.ds(j * 2 * EHD, 2 * EHD)
        total = None
        for e in range(2):
            keys = jnp.where(feature == e, mem[0, lines], jnp.bfloat16(0))
            vals = jnp.where(feature == e, mem[1, lines], jnp.bfloat16(0))
            scores = dot(query[:, lines], keys) * (1.0 / math.sqrt(EHD))
            term = dot(weigh(scores, mask), vals, ((1,), (1,)))
            total = term if e == 0 else total + term
        mixed[:, lines] = total.astype(jnp.bfloat16)
    branch = dot(mixed[...], wo[...])
    enc[head] = rms_rows(cop[...].astype(jnp.float32) + branch).astype(jnp.bfloat16)
    enc_copy = remote(enc.at[head], enc.at[head], enc_sem.at[0], enc_sem.at[1], head=other)
    go(enc_copy)
    w_chunk = w_in.shape[0] // W_CUTS

    def w_part(side, i):
        lines = (1 - side) * i + side * (W_CUTS - 1 - i)
        return pl.ds(pl.multiple_of(lines * w_chunk, 16), w_chunk)

    w_pairs = []
    for i in range(W_CUTS - W_CROSS):
        lines = w_part(plane, i)
        w_pairs.append(remote(
            w_in.at[lines], w_all.at[y, lines], wy_sem.at[0, i], wy_sem.at[1, i], span=2 * z + 1 - y,
        ))

    def w_forward(i):
        w_pairs[i].wait_recv()
        spot = w_all.at[1 - y, w_part(plane, i)]
        go(remote(spot, spot, wx_sem.at[0, i], wx_sem.at[1, i], groups=twin))

    def w_arrival(i):
        spot = w_all.at[1 - y, w_part(1 - plane, i)]
        remote(spot, spot, wx_sem.at[0, i], wx_sem.at[1, i], groups=twin).wait_recv()

    def far_lines():
        for k in range(3, length):
            line_arrival(k, note=False)
    pl.when(inner)(far_lines)
    enc_copy.wait_recv()

    loads[1].wait()
    asks = ask_ref.shape[0]
    def send_attended(place):
        spot = pl.ds(2 * place, 2)
        for travel in (1, -1):
            nxt = z + travel
            lane = (1 - travel) // 2
            copy = remote(
                att_ref.at[spot], gathered.at[z, spot], att_sem.at[0, lane, z, place], att_sem.at[1, lane, z, place],
                span=2 * ((nxt + length) % length) + y,
            )
            go(copy, (nxt >= 0) & (nxt < length))

    dec_mask = same_span((asks, NB * rows), CT, PT, spans)

    def attend(block):
        flat = enc[...].reshape(NB * rows, width)
        keys = dot(flat, kvg[block, :, pl.ds(0, HD)]).astype(jnp.bfloat16)
        vals = dot(flat, kvg[block, :, pl.ds(HD, HD)]).astype(jnp.bfloat16)
        spot = pl.ds(pl.multiple_of(block * HD, HD), HD)
        scores = dot(ask_ref[:, spot], keys, ((1,), (1,))) * (1.0 / math.sqrt(HD))
        att_ref[block] = dot(weigh(scores, dec_mask), vals).astype(jnp.bfloat16)

    for j in range(length):
        source = line_order(z, length, j)[0] if j else z
        blocks = [2 * source + y, 2 * source + 1 - y]
        for block in blocks[0 if j else 1:]:
            twin_arrival(block)
        for block in blocks:
            attend(block)
        send_attended(source)
        if j == length - 1:
            for i in range(W_CROSS):
                w_forward(i)
        if j == 0:
            pl.when(jnp.logical_not(inner))(far_lines)
            for k in range(3, length):
                line_arrival(k, start=False)
                pair_arrival(k - 1)
            for copy in w_pairs:
                go(copy)
        if j == 1:
            pair_arrival(length - 1)

    owner_head = z // (length // 2)
    column = z % (length // 2)
    out_rows = asks // 2
    w_width = w_in.shape[1]
    crossings, returns = [], []

    def attended_arrival(j, start=True, note=True):
        source, travel = line_order(z, length, j, 1)
        lane = (1 - travel) // 2
        nxt = z + travel
        for i in range(length):
            place = line_order(source, length, i)[0] if i else source
            slot = gathered.at[source, pl.ds(2 * place, 2)]
            copy = remote(
                slot, slot, att_sem.at[0, lane, source, place], att_sem.at[1, lane, source, place],
                span=2 * ((nxt + length) % length) + y,
            )
            if start:
                copy.wait_recv()
            go(copy, (nxt >= 0) & (nxt < length), start=start, note=note)

    def project(slot, k, rows_ref, place):
        whole = jnp.concatenate([rows_ref[m] for m in range(n)], axis=1)
        value = dot(whole, w_all[k]).astype(jnp.bfloat16)
        partial[slot, k, 0] = value[:out_rows]
        partial[slot, k, 1] = value[out_rows:]
        copy = remote(
            partial.at[slot, k, other], crossed.at[slot, k], cross_sem.at[0, slot, k], cross_sem.at[1, slot, k], head=other,
        )
        go(copy)
        crossings.append((copy, slot, k, place))

    def give_back():
        copy, slot, k, place = crossings[len(returns)]
        copy.wait_recv()
        total = partial[slot, k, head].astype(jnp.float32) + crossed[slot, k].astype(jnp.float32)
        summed[slot, k] = total.astype(jnp.bfloat16)
        copy = remote(
            summed.at[slot, k], back.at[column, head, k], send_sem.at[slot, k], back_sem.at[column, head, k],
            span=2 * place + y, head=owner_head,
        )
        if slot == 0:
            @pl.when(head == owner_head)
            def _():
                back[column, head, k] = summed[slot, k]

            go(copy, head != owner_head)
        else:
            go(copy)
        returns.append(copy)

    loads[2].wait()
    loads[3].wait()
    arrived = [(att_ref, z)]

    for j in range(1, length):
        source = line_order(z, length, j, 1)[0]
        arrived.append((gathered.at[source], source))

    def last_arrival():
        attended_arrival(length - 1, note=False)

    def work(slot, k):
        project(slot, k, *arrived[slot])
        if len(crossings) > 1:
            give_back()
    work(0, y)
    for j in range(1, length - 1):
        attended_arrival(j)
        work(j, y)
    pl.when(inner)(last_arrival)
    for i in range(W_CROSS, W_CUTS - W_CROSS):
        w_pairs[i].wait_recv()
    for i in range(W_CROSS):
        w_arrival(i)
    for j in range(length - 1):
        work(j, 1 - y)
    pl.when(jnp.logical_not(inner))(last_arrival)
    attended_arrival(length - 1, start=False)
    work(length - 1, y)
    work(length - 1, 1 - y)
    give_back()

    stored = []
    for j in range(length // 2):
        for source in range(2):
            for k in range(2):
                local = (head * (length // 2) + j == z) & (head == source)

                @pl.when(jnp.logical_not(local))
                def _():
                    remote(
                        summed.at[0, 0], back.at[j, source, k], send_sem.at[0, 0], back_sem.at[j, source, k], head=other,
                    ).wait_recv()

                lanes = pl.ds((2 * j + k) * w_width, w_width)
                lines = pl.ds(source * out_rows, out_rows)
                states_ref[lines, lanes] = (
                    states_ref[lines, lanes].astype(jnp.float32) + back[j, source, k].astype(jnp.float32)
                ).astype(jnp.bfloat16)
                copy = pltpu.make_async_copy(
                    states_ref.at[lines, lanes], out_ref.at[lines, lanes], local_sem.at[11 + len(stored)],
                )
                copy.start()
                stored.append(copy)
    for copy in stored:
        copy.wait()
    for copy, cond in pending:
        if cond is None:
            copy.wait_send()
        else:
            pl.when(cond)(copy.wait_send)


def out_kernel(n, *refs):
    barrier, greeted = greet_all(n)
    pl.semaphore_wait(barrier, greeted)
    out_stage(n, *refs)


def out_stage(
    n, att_ref, w_ref, states_ref, out_ref,
    gathered, part, crossed, summed, back, ring_sem, cross_sem, send_sem, back_sem,
):
    me = lax.axis_index("span")
    head = lax.axis_index("head")
    other = 1 - head
    half = n // 2
    owner_head = me // half
    column = me % half
    rows = att_ref.shape[0]
    half_rows = rows // 2
    width = w_ref.shape[1]

    def pieces(ref):
        return [ref.at[pl.ds(k * half_rows, half_rows)] for k in range(2)]

    ring = Ring(n, pieces(att_ref), lambda block: pieces(gathered.at[block]), ring_sem)
    ring.start()
    crossings, returns = [], []

    def project(block, rows_ref):
        i = len(crossings)
        value = jnp.dot(rows_ref[...], w_ref[...], preferred_element_type=jnp.float32)
        value = value.astype(jnp.bfloat16)
        part[i, 0] = value[:half_rows]
        part[i, 1] = value[half_rows:]
        copy = remote(part.at[i, other], crossed.at[i], cross_sem.at[0, i], cross_sem.at[1, i], head=other)
        crossings.append((copy, block))

    def send_across():
        crossings[-1][0].start()

    def give_back():
        i = len(returns)
        copy, block = crossings[i]
        copy.wait_recv()
        total = part[i, head].astype(jnp.float32) + crossed[i].astype(jnp.float32)
        summed[i] = total.astype(jnp.bfloat16)
        copy = remote(
            summed.at[i], back.at[column, head], send_sem.at[i], back_sem.at[column, head],
            span=block, head=owner_head,
        )
        if i == 0:
            @pl.when(head != owner_head)
            def _():
                copy.start()

            @pl.when(head == owner_head)
            def _():
                back[column, head] = summed[i]
        else:
            copy.start()
        returns.append(copy)

    project(me, att_ref)
    send_across()
    for t in range(ring.steps):
        for block in ring.advance(t):
            project(block, gathered.at[block])
            send_across()
            give_back()
    give_back()

    for j in range(half):
        for source in range(2):
            mine = (head * half + j == me) & (head == source)

            @pl.when(jnp.logical_not(mine))
            def _():
                remote(
                    summed.at[0], back.at[j, source], send_sem.at[0], back_sem.at[j, source], head=other,
                ).wait_recv()

            lanes = pl.ds(j * width, width)
            lines = pl.ds(source * half_rows, half_rows)
            out_ref[lines, lanes] = (
                states_ref[lines, lanes].astype(jnp.float32) + back[j, source].astype(jnp.float32)
            ).astype(jnp.bfloat16)
    ring.finish()
    for copy, _ in crossings:
        copy.wait_send()
    for i, copy in enumerate(returns):
        if i == 0:
            @pl.when(head != owner_head)
            def _():
                copy.wait_send()
        else:
            copy.wait_send()


def call(kernel, collective_id, out_shape, scratch_shapes, spaces, *operands, out_space=pltpu.VMEM):
    return pl.pallas_call(
        kernel,
        out_shape=out_shape,
        in_specs=[pl.BlockSpec(memory_space=space) for space in spaces],
        out_specs=[pl.BlockSpec(memory_space=out_space)] * len(out_shape),
        scratch_shapes=scratch_shapes,
        compiler_params=pltpu.CompilerParams(collective_id=collective_id, has_side_effects=True),
    )(*operands)


def decode(encoded, kv_all, span_queries, span_count):
    dec_kv = jnp.einsum(
        "re,nsec->rsnc", encoded.reshape(-1, E), kv_all, preferred_element_type=jnp.float32
    ).astype(jnp.bfloat16)
    head_count = span_queries.shape[1] // HD
    dec_kv = dec_kv.reshape(NB, span_count, PT, 2, head_count, HD)
    dec_query = span_queries.reshape(span_count, CT, head_count, HD)
    scores = jnp.einsum(
        "cqhd,ncphd->chqnp", dec_query, dec_kv[:, :, :, 0], preferred_element_type=jnp.float32
    ) / math.sqrt(HD)
    scores = scores.reshape(span_count, head_count, CT, NB * PT)
    weights = softmax_rows(scores).astype(jnp.bfloat16)
    weights = weights.reshape(span_count, head_count, CT, NB, PT)
    attended = jnp.einsum(
        "chqnp,ncphd->cqhd", weights, dec_kv[:, :, :, 1], preferred_element_type=jnp.float32
    )
    return attended.astype(jnp.bfloat16).reshape(span_count * CT, head_count * HD)


def body(
    span_states,
    span_queries,
    span_memory,
    passages,
    neighbours,
    enc_query_w,
    enc_out_w,
    kv_weight,
    out_weight,
):
    n = lax.axis_size("span")
    span_count = neighbours.shape[0]
    bf16 = jnp.bfloat16
    dma = pltpu.SemaphoreType.DMA
    half_rows = PT // 2
    memory = span_memory.transpose(1, 2, 0)
    rows, tokens = span_count * PT, span_memory.shape[0]
    sds = jax.ShapeDtypeStruct
    states, width = sds(span_states.shape, bf16), out_weight.shape[1]
    half = tokens // 2
    operands = (neighbours, passages.reshape(-1, 2, half_rows, E), memory, enc_query_w.T, enc_out_w.T)
    pas_scratch = [pltpu.VMEM((passages.shape[0] // PT, 2, half_rows, E), bf16)]
    scratch = [
        pltpu.VMEM((8, 128), jnp.int32),
        pltpu.VMEM((n, 8, 128), jnp.int32),
        pltpu.SMEM((n, 8, 128), jnp.int32),
        pltpu.VMEM((n, half_rows, E), bf16),
        pltpu.VMEM((n, half_rows, E), bf16),
        pltpu.VMEM((span_count, half_rows, E), bf16),
        pltpu.VMEM((rows, E), bf16),
        pltpu.VMEM((2, E, tokens), bf16),
        pltpu.VMEM((E, E), bf16),
        pltpu.VMEM((E, E), bf16),
        pltpu.VMEM((rows, E), bf16),
        pltpu.VMEM((rows, E), bf16),
        dma((11 + 4 * n,)),
        dma((2, n)),
        dma((2, n)),
        dma((2, span_count)),
        dma((2, 4)),
        dma((2,)),
    ]
    if kv_weight.shape[2] == HD and n % 4 == 0:
        length = n // 2
        line_scratch = [
            pltpu.VMEM((NB, rows, E), bf16),
            pltpu.VMEM((n, E, 2 * HD), bf16),
            pltpu.VMEM((n, tokens, HD), bf16),
            pltpu.VMEM((2,) + out_weight.shape, bf16),
            pltpu.VMEM(span_states.shape, bf16),
            pltpu.VMEM((length, n, tokens, HD), bf16),
            pltpu.VMEM((length, 2, 2, half, width), bf16),
            pltpu.VMEM((length, 2, half, width), bf16),
            pltpu.VMEM((length, 2, half, width), bf16),
            pltpu.VMEM((length // 2, 2, 2, half, width), bf16),
        ]
        line_sems = [
            dma((2, length, 2, KV_CUTS)),
            dma((2, length, KV_CUTS)),
            dma((2, n, KV_CUTS)),
            dma((2, W_CUTS)),
            dma((2, W_CUTS)),
            dma((2, 2, length, length)),
            dma((2, length, 2)),
            dma((length, 2)),
            dma((length // 2, 2, 2)),
        ]
        return call(
            functools.partial(span_kernel, n, span_count), 2, [states],
            line_scratch + pas_scratch + [pltpu.VMEM(span_queries.shape, bf16)] + scratch + line_sems,
            [pltpu.VMEM] + [pl.ANY] * 8,
            *operands, kv_weight.reshape(E, 2 * HD), span_queries, out_weight, span_states,
            out_space=pl.ANY,
        )[0]
    kv = kv_weight.transpose(1, 0, 2)
    out_scratch = [
        pltpu.VMEM((n,) + span_queries.shape, bf16),
        pltpu.VMEM((n, 2, half, width), bf16),
        pltpu.VMEM((n, half, width), bf16),
        pltpu.VMEM((n, half, width), bf16),
        pltpu.VMEM((n // 2, 2, half, width), bf16),
        dma((2, 2, n // 2, 2)),
        dma((2, n)),
        dma((n,)),
        dma((n // 2, 2)),
    ]
    found = call(
        functools.partial(fetch_kernel, n, span_count), 0,
        [sds((NB, rows, E), bf16), sds((n,) + kv.shape, bf16)],
        pas_scratch + scratch + [dma((2, 2, n // 2, 4)), dma((2, 2, n // 2, 2))], [pltpu.VMEM] + [pl.ANY] * 5,
        *operands, kv,
    )
    attended = decode(found[0], found[1], span_queries, span_count)
    return call(
        functools.partial(out_kernel, n), 1, [states], out_scratch, [pltpu.VMEM] * 3,
        attended, out_weight, span_states,
    )[0]


def solution(mesh):
    placed = (
        P(("groups", "span"), "head"),
        P(("groups", "span"), "head"),
        P(("groups", "span"), None, "head"),
        P(("groups", "span"), None),
        P(("groups", "span"), None),
        P(None, "head"),
        P(None, "head"),
        P(None, None, ("head", "span")),
        P("head", "span"),
    )
    return jax.shard_map(
        body, mesh=mesh, in_specs=placed, out_specs=P(("groups", "span"), "head"), check_vma=False
    )
```

```python
import functools
import math

import jax
import jax.numpy as jnp
from jax import lax
from jax.experimental import pallas as pl
from jax.experimental.pallas import tpu as pltpu
from jax.sharding import PartitionSpec as P

HD = 128
E = 896
EHD = 64
CT = 64
PT = 128
NB = 2
PS_DEV = 8
MESH = pl.DeviceIdType.MESH


epsilon = 1e-06


def rms_rows(values):
    return values * lax.rsqrt(jnp.mean(values * values, axis=-1, keepdims=True) + epsilon)


def softmax_rows(scores):
    top_score = jnp.max(scores, axis=-1, keepdims=True)
    raised = jnp.exp(scores - top_score)
    return raised / jnp.sum(raised, axis=-1, keepdims=True)


def ring_place(span, n):
    odd = span % 2
    return (1 - odd) * (span // 2) + odd * (n - 1 - span // 2)


def ring_span(place, n):
    back = place // (n // 2)
    return (1 - back) * (2 * place) + back * (2 * (n - 1 - place) + 1)


def remote(src, dst, send_sem, recv_sem, **where):
    return pltpu.make_async_remote_copy(
        src_ref=src, dst_ref=dst, send_sem=send_sem, recv_sem=recv_sem,
        device_id=where, device_id_type=MESH,
    )


class Ring:
    def __init__(self, n, own, slots, sems):
        me = lax.axis_index("span")
        self.n, self.own, self.slots, self.sems = n, own, slots, sems
        self.place = ring_place(me, n)
        self.targets = (ring_span((self.place + 1) % n, n), ring_span((self.place + n - 1) % n, n))
        self.steps = n // 2
        self.copies = {}

    def travels(self, t, side, k):
        return t < self.steps - 1 or k % 2 == side

    def block(self, t, side):
        n = self.n
        return ring_span((self.place + (n - t if side == 0 else t)) % n, n)

    def send(self, t, side, k):
        dst = self.slots(self.block(t, side))[k]
        copy = remote(
            self.own[k] if t == 0 else dst, dst,
            self.sems.at[0, side, t, k], self.sems.at[1, side, t, k], span=self.targets[side],
        )
        copy.start()
        self.copies[t, side, k] = copy

    def start(self):
        for k in range(len(self.own)):
            for side in range(2):
                if self.travels(0, side, k):
                    self.send(0, side, k)

    def advance(self, t, forward=None):
        for k in range(len(self.own)):
            for side in range(2):
                if self.travels(t, side, k):
                    self.copies[t, side, k].wait_recv()
                    if t + 1 < self.steps and self.travels(t + 1, side, k):
                        self.send(t + 1, side, k)
                    if forward is not None:
                        forward(t, side, k, self.block(t + 1, side))
        return [self.block(t + 1, side) for side in range(1 if t == self.steps - 1 else 2)]

    def finish(self):
        for copy in self.copies.values():
            copy.wait_send()


def weigh(scores, mask):
    scores = jnp.where(mask, scores, -jnp.inf)
    raised = jnp.exp(scores - jnp.max(scores, axis=-1, keepdims=True))
    return (raised * (1.0 / jnp.sum(raised, axis=-1, keepdims=True))).astype(jnp.bfloat16)


def same_span(shape, rows_each, lanes_each, spans):
    row = lax.broadcasted_iota(jnp.int32, shape, 0) // rows_each
    lane = (lax.broadcasted_iota(jnp.int32, shape, 1) // lanes_each) % spans
    return row == lane


def dot(a, b, dims=((1,), (0,))):
    return lax.dot_general(a, b, (dims, ((), ())), preferred_element_type=jnp.float32)


def greet_all(n):
    me = lax.axis_index("span")
    head = lax.axis_index("head")
    barrier = pltpu.get_barrier_semaphore()
    for d in range(n):
        for hop in range(2):
            if d or hop:
                pl.semaphore_signal(
                    barrier, inc=1,
                    device_id={"span": (me + d) % n, "head": (head + hop) % 2}, device_id_type=MESH,
                )
    return barrier, 2 * n - 1


def fetch_kernel(
    n, spans, nb_ref, pas_in, mem_ref, wq_ref, wo_ref, kv_ref, enc, kvg,
    pas_ref, nb_own, nbg, nbs, picks, got, swap, cop, mem, wq, wo, query, mixed,
    local_sem, nb_sem, pas_sem, swap_sem, w_sem, enc_sem, ring_sem, twin_sem,
):
    me = lax.axis_index("span")
    head = lax.axis_index("head")
    group = lax.axis_index("groups")
    other = 1 - head
    twin = group + 1 - 2 * (group % 2)
    part = group % 2
    half_rows = PT // 2
    half_e = wq_ref.shape[0]
    barrier, greeted = greet_all(n)
    pl.semaphore_signal(barrier, inc=1, device_id={"groups": twin}, device_id_type=MESH)
    loads = [pltpu.make_async_copy(pas_in, pas_ref, local_sem.at[7])]
    for copy in loads:
        copy.start()
    nb_own[...] = jnp.zeros_like(nb_own)
    nb_own[:spans, :NB] = nb_ref[...]
    pl.semaphore_wait(barrier, greeted + 1)

    nb_copies = []
    for d in range(1, n):
        copy = remote(nb_own, nbg.at[me], nb_sem.at[0, d], nb_sem.at[1, d], span=(me + d) % n)
        copy.start()
        nb_copies.append(copy)
    own_nb = pltpu.make_async_copy(nb_own, nbg.at[me], local_sem.at[0])
    own_nb.start()

    depth = kv_ref.shape[1]
    half, extra = depth // 2, depth // 28 * 3
    near, far = part, 1 - part

    def pieces(ref):
        return [
            ref.at[near, pl.ds(0, half)], ref.at[near, pl.ds(half, half)],
            ref.at[far, pl.ds(0, extra // 2)], ref.at[far, pl.ds(extra // 2, extra // 2)],
        ]

    ring = Ring(n, pieces(kv_ref), lambda block: pieces(kvg.at[block]), ring_sem)
    twins = [[] for _ in range(ring.steps)]

    def to_twin(t, side, k, block):
        if k < 2:
            lines = pl.ds(extra, half - extra) if k == 0 else pl.ds(half, half)
            piece = kvg.at[block, near, lines]
            copy = remote(piece, piece, twin_sem.at[0, side, t, k], twin_sem.at[1, side, t, k], groups=twin)
            copy.start()
            twins[t].append(copy)

    ring.start()
    mine = pl.ds(pl.multiple_of(head * half_e, half_e), half_e)
    w_copies, own_copies = [], []
    for i, (src, dst) in enumerate((
        (mem_ref.at[0], mem.at[0, mine]), (mem_ref.at[1], mem.at[1, mine]), (wq_ref, wq.at[mine]), (wo_ref, wo.at[mine]),
    )):
        w_copies.append(remote(src, dst, w_sem.at[0, i], w_sem.at[1, i], head=other))
        w_copies[-1].start()
        own_copies.append(pltpu.make_async_copy(src, dst, local_sem.at[3 + i]))
        own_copies[-1].start()
    own_copies.append(pltpu.make_async_copy(kv_ref, kvg.at[me], local_sem.at[1]))
    own_copies[-1].start()
    own_nb.wait()
    loads[0].wait()
    for copy in nb_copies:
        copy.wait()
    to_scalar = pltpu.make_async_copy(nbg, nbs, local_sem.at[2])
    to_scalar.start()
    to_scalar.wait()

    def pick(requester):
        index = jnp.int32(0)
        for e in range(spans * NB):
            wanted = nbs[requester, e // NB, e % NB]
            index = index + jnp.where(wanted // PS_DEV == me, wanted % PS_DEV, 0)
        return pas_ref[index, head]

    pas_copies = []
    picks[1] = pick((me + 1) % n)
    for d in range(1, n):
        if d + 1 < n:
            picks[d + 1] = pick((me + d + 1) % n)
        else:
            got[me] = pick(me)
        copy = remote(picks.at[d], got.at[me], pas_sem.at[0, d], pas_sem.at[1, d], span=(me + d) % n)
        copy.start()
        pas_copies.append(copy)

    arrivals = [ring.advance(0, to_twin)]
    for copy in pas_copies:
        copy.wait_recv()
    swaps = []
    for c in range(spans):
        swap[c] = got[nbs[me, c, other] // PS_DEV]
    for c in range(spans):
        spot = cop.at[pl.ds(pl.multiple_of(c * PT + head * half_rows, half_rows), half_rows)]
        copy = remote(swap.at[c], spot, swap_sem.at[0, c], swap_sem.at[1, c], head=other)
        copy.start()
        swaps.append(copy)
        spot[...] = got[nbs[me, c, head] // PS_DEV]
    for copy in own_copies:
        copy.wait()
    for copy in w_copies:
        copy.wait()
    for copy in swaps:
        copy.wait()

    arrivals.append(ring.advance(1, to_twin))
    rows = cop.shape[0]
    tokens = mem.shape[2]
    width = cop.shape[1]
    values = cop[...].astype(jnp.float32)
    query[...] = dot(rms_rows(values).astype(jnp.bfloat16), wq[...], ((1,), (1,))).astype(jnp.bfloat16)
    mask = same_span((rows, tokens), PT, CT, spans)
    feature = lax.broadcasted_iota(jnp.int32, (2 * EHD, tokens), 0) // EHD
    for j in range(width // (2 * EHD)):
        lines = pl.ds(j * 2 * EHD, 2 * EHD)
        total = None
        for e in range(2):
            keys = jnp.where(feature == e, mem[0, lines], jnp.bfloat16(0))
            vals = jnp.where(feature == e, mem[1, lines], jnp.bfloat16(0))
            scores = dot(query[:, lines], keys) * (1.0 / math.sqrt(EHD))
            term = dot(weigh(scores, mask), vals, ((1,), (1,)))
            total = term if e == 0 else total + term
        mixed[:, lines] = total.astype(jnp.bfloat16)
    branch = dot(mixed[...], wo[...])
    enc[head] = rms_rows(cop[...].astype(jnp.float32) + branch).astype(jnp.bfloat16)
    enc_copy = remote(enc.at[head], enc.at[head], enc_sem.at[0], enc_sem.at[1], head=other)
    enc_copy.start()
    if ring.steps > 2:
        arrivals.append(ring.advance(2, to_twin))
    enc_copy.wait_recv()

    for t in range(ring.steps):
        while len(arrivals) < min(t + 3, ring.steps):
            arrivals.append(ring.advance(len(arrivals), to_twin))
        for copy in twins[t]:
            copy.wait_recv()
    enc_copy.wait_send()
    for copy in pas_copies + [copy for pair in twins for copy in pair]:
        copy.wait_send()
    ring.finish()


W_CUTS = 4
W_CROSS = 1
KV_EXTRA = 6
KV_CUTS = 2


def line_order(z, length, j, first=-1):
    far_half = z // max(1, length // 2)
    short = (1 - far_half) * z + far_half * (length - 1 - z)
    way = 1 - 2 * far_half
    both = (2 * short - j + 2 * length) // (2 * length)
    turn = first * (2 * (j % 2) - 1)
    source = z + both * turn * way * ((j + 1) // 2) + (1 - both) * way * (j - short)
    travel = -(both * turn * way + (1 - both) * way)
    return source, travel


def span_kernel(
    n, spans, nb_ref, pas_in, mem_ref, wq_ref, wo_ref, kv_ref, ask_in, w_in, states_in, out_ref,
    enc, kvg, att_ref, w_all, states_ref, gathered, partial, crossed, summed, back,
    kv_rows, kv_wide, pas_ref, ask_ref, nb_own, nbg, nbs, picks, got, swap, cop, mem, wq, wo, query, mixed,
    local_sem, nb_sem, pas_sem, swap_sem, w_sem, enc_sem, kvz_sem, kvy_sem, kvx_sem,
    wy_sem, wx_sem, att_sem, cross_sem, send_sem, back_sem,
):
    me = lax.axis_index("span")
    head = lax.axis_index("head")
    group = lax.axis_index("groups")
    other = 1 - head
    twin = group + 1 - 2 * (group % 2)
    plane = group % 2
    length = n // 2
    z, y = me // 2, me % 2
    half_rows = PT // 2
    half_e = wq_ref.shape[0]
    pending = []

    def go(copy, cond=None, start=True, note=True):
        if start:
            if cond is None:
                copy.start()
            else:
                pl.when(cond)(copy.start)
        if note:
            pending.append((copy, cond))

    barrier, greeted = greet_all(n)
    pl.semaphore_signal(barrier, inc=1, device_id={"groups": twin}, device_id_type=MESH)
    depth = kv_ref.shape[0] // 2
    kv_load = pltpu.make_async_copy(kv_ref, kv_rows, local_sem.at[1])
    kv_load.start()
    loads = [
        pltpu.make_async_copy(pas_in, pas_ref, local_sem.at[7]),
        pltpu.make_async_copy(ask_in, ask_ref, local_sem.at[8]),
        pltpu.make_async_copy(w_in, w_all.at[y], local_sem.at[9]),
        pltpu.make_async_copy(states_in, states_ref, local_sem.at[10]),
    ]
    for copy in loads:
        copy.start()
    nb_own[...] = jnp.zeros_like(nb_own)
    nb_own[:spans, :NB] = nb_ref[...]
    kv_load.wait()
    kv_wide[...] = kv_rows[...].astype(jnp.float32)
    for i in range(2):
        kvg[me, :, pl.ds(i * HD, HD)] = kv_wide[pl.ds(i, depth, stride=2)].astype(jnp.bfloat16)
    pl.semaphore_wait(barrier, greeted + 1)

    for d in range(1, n):
        go(remote(nb_own, nbg.at[me], nb_sem.at[0, d], nb_sem.at[1, d], span=(me + d) % n))
    own_nb = pltpu.make_async_copy(nb_own, nbg.at[me], local_sem.at[0])
    own_nb.start()

    half, extra = depth // 2, depth // 56 * KV_EXTRA
    cut = (half + extra) // KV_CUTS
    parts = range(KV_CUTS)

    def from_edge(side, offset, size):
        return pl.ds(pl.multiple_of((1 - side) * offset + side * (depth - offset - size), 16), size)

    def plane_part(i):
        return from_edge(plane, i * cut, cut)

    def cross_part(side, i):
        start = min(i * cut, half - extra)
        return from_edge(side, start, min((i + 1) * cut, half - extra) - start)

    crossed_parts = [i for i in parts if i * cut < half - extra]

    def along(source, travel, i, **how):
        lines = plane_part(i)
        spot = kvg.at[2 * source + y, lines]
        nxt = z + travel
        lane = (1 - travel) // 2
        copy = remote(
            spot, spot, kvz_sem.at[0, source, lane, i], kvz_sem.at[1, source, lane, i],
            span=2 * ((nxt + length) % length) + y,
        )
        go(copy, (nxt >= 0) & (nxt < length), **how)

    def to_pair(source, i, **how):
        lines = plane_part(i)
        spot = kvg.at[2 * source + y, lines]
        go(remote(
            spot, spot, kvy_sem.at[0, source, i], kvy_sem.at[1, source, i],
            span=2 * z + 1 - y,
        ), **how)

    def to_twin(block, i, **how):
        if i in crossed_parts:
            spot = kvg.at[block, cross_part(plane, i)]
            go(remote(spot, spot, kvx_sem.at[0, block, i], kvx_sem.at[1, block, i], groups=twin), **how)

    def line_arrival(j, start=True, note=True):
        source, travel = line_order(z, length, j)
        lane = (1 - travel) // 2
        block = 2 * source + y
        for i in parts:
            spot = kvg.at[block, plane_part(i)]
            if start:
                remote(
                    spot, spot, kvz_sem.at[0, source, lane, i], kvz_sem.at[1, source, lane, i], span=2 * z + 1 - y,
                ).wait_recv()
            along(source, travel, i, start=start, note=note)
            to_pair(source, i, start=start, note=note)
            to_twin(block, i, start=start, note=note)

    def pair_arrival(j):
        source = z if j == 0 else line_order(z, length, j)[0]
        block = 2 * source + 1 - y
        for i in parts:
            spot = kvg.at[block, plane_part(i)]
            remote(spot, spot, kvy_sem.at[0, source, i], kvy_sem.at[1, source, i], span=2 * z + 1 - y).wait_recv()
            to_twin(block, i)

    def twin_arrival(block):
        for i in crossed_parts:
            spot = kvg.at[block, cross_part(1 - plane, i)]
            remote(spot, spot, kvx_sem.at[0, block, i], kvx_sem.at[1, block, i], groups=twin).wait_recv()

    for i in parts:
        for travel in (1, -1):
            along(z, travel, i)
        to_pair(z, i)

    mine = pl.ds(pl.multiple_of(head * half_e, half_e), half_e)
    w_copies, own_copies = [], []
    for i, (src, dst) in enumerate((
        (mem_ref.at[0], mem.at[0, mine]), (mem_ref.at[1], mem.at[1, mine]), (wq_ref, wq.at[mine]), (wo_ref, wo.at[mine]),
    )):
        w_copies.append(remote(src, dst, w_sem.at[0, i], w_sem.at[1, i], head=other))
        w_copies[-1].start()
        own_copies.append(pltpu.make_async_copy(src, dst, local_sem.at[3 + i]))
        own_copies[-1].start()
    own_nb.wait()
    loads[0].wait()
    for d in range(1, n):
        pending[d - 1][0].wait_recv()
    to_scalar = pltpu.make_async_copy(nbg, nbs, local_sem.at[2])
    to_scalar.start()
    to_scalar.wait()

    def pick(requester):
        index = jnp.int32(0)
        for e in range(spans * NB):
            wanted = nbs[requester, e // NB, e % NB]
            index = index + jnp.where(wanted // PS_DEV == me, wanted % PS_DEV, 0)
        return pas_ref[index, head]

    pas_copies = []
    picks[1] = pick((me + 1) % n)
    for d in range(1, n):
        if d + 1 < n:
            picks[d + 1] = pick((me + d + 1) % n)
        else:
            got[me] = pick(me)
        copy = remote(picks.at[d], got.at[me], pas_sem.at[0, d], pas_sem.at[1, d], span=(me + d) % n)
        go(copy)
        pas_copies.append(copy)
    line_arrival(1)
    pair_arrival(0)
    inner = (z > 0) & (z < length - 1)
    pl.when(inner)(lambda: line_arrival(2, note=False))
    for copy in pas_copies:
        copy.wait_recv()
    swaps = []
    for c in range(spans):
        swap[c] = got[nbs[me, c, other] // PS_DEV]
    for c in range(spans):
        spot = cop.at[pl.ds(pl.multiple_of(c * PT + head * half_rows, half_rows), half_rows)]
        copy = remote(swap.at[c], spot, swap_sem.at[0, c], swap_sem.at[1, c], head=other)
        copy.start()
        swaps.append(copy)
        spot[...] = got[nbs[me, c, head] // PS_DEV]
    pl.when(jnp.logical_not(inner))(lambda: line_arrival(2, note=False))
    line_arrival(2, start=False)
    pair_arrival(1)
    for copy in own_copies:
        copy.wait()
    for copy in w_copies:
        copy.wait()
    for copy in swaps:
        copy.wait()
    rows = cop.shape[0]
    tokens = mem.shape[2]
    width = cop.shape[1]
    values = cop[...].astype(jnp.float32)
    query[...] = dot(rms_rows(values).astype(jnp.bfloat16), wq[...], ((1,), (1,))).astype(jnp.bfloat16)
    mask = same_span((rows, tokens), PT, CT, spans)
    feature = lax.broadcasted_iota(jnp.int32, (2 * EHD, tokens), 0) // EHD
    for j in range(width // (2 * EHD)):
        lines = pl.ds(j * 2 * EHD, 2 * EHD)
        total = None
        for e in range(2):
            keys = jnp.where(feature == e, mem[0, lines], jnp.bfloat16(0))
            vals = jnp.where(feature == e, mem[1, lines], jnp.bfloat16(0))
            scores = dot(query[:, lines], keys) * (1.0 / math.sqrt(EHD))
            term = dot(weigh(scores, mask), vals, ((1,), (1,)))
            total = term if e == 0 else total + term
        mixed[:, lines] = total.astype(jnp.bfloat16)
    branch = dot(mixed[...], wo[...])
    enc[head] = rms_rows(cop[...].astype(jnp.float32) + branch).astype(jnp.bfloat16)
    enc_copy = remote(enc.at[head], enc.at[head], enc_sem.at[0], enc_sem.at[1], head=other)
    go(enc_copy)
    w_chunk = w_in.shape[0] // W_CUTS

    def w_part(side, i):
        lines = (1 - side) * i + side * (W_CUTS - 1 - i)
        return pl.ds(pl.multiple_of(lines * w_chunk, 16), w_chunk)

    w_pairs = []
    for i in range(W_CUTS - W_CROSS):
        lines = w_part(plane, i)
        w_pairs.append(remote(
            w_in.at[lines], w_all.at[y, lines], wy_sem.at[0, i], wy_sem.at[1, i], span=2 * z + 1 - y,
        ))

    def w_forward(i):
        w_pairs[i].wait_recv()
        spot = w_all.at[1 - y, w_part(plane, i)]
        go(remote(spot, spot, wx_sem.at[0, i], wx_sem.at[1, i], groups=twin))

    def w_arrival(i):
        spot = w_all.at[1 - y, w_part(1 - plane, i)]
        remote(spot, spot, wx_sem.at[0, i], wx_sem.at[1, i], groups=twin).wait_recv()

    def far_lines():
        for k in range(3, length):
            line_arrival(k, note=False)
    pl.when(inner)(far_lines)
    enc_copy.wait_recv()

    loads[1].wait()
    asks = ask_ref.shape[0]
    def send_attended(place):
        spot = pl.ds(2 * place, 2)
        for travel in (1, -1):
            nxt = z + travel
            lane = (1 - travel) // 2
            copy = remote(
                att_ref.at[spot], gathered.at[z, spot], att_sem.at[0, lane, z, place], att_sem.at[1, lane, z, place],
                span=2 * ((nxt + length) % length) + y,
            )
            go(copy, (nxt >= 0) & (nxt < length))

    dec_mask = same_span((asks, NB * rows), CT, PT, spans)

    def attend(block):
        flat = enc[...].reshape(NB * rows, width)
        keys = dot(flat, kvg[block, :, pl.ds(0, HD)]).astype(jnp.bfloat16)
        vals = dot(flat, kvg[block, :, pl.ds(HD, HD)]).astype(jnp.bfloat16)
        spot = pl.ds(pl.multiple_of(block * HD, HD), HD)
        scores = dot(ask_ref[:, spot], keys, ((1,), (1,))) * (1.0 / math.sqrt(HD))
        att_ref[block] = dot(weigh(scores, dec_mask), vals).astype(jnp.bfloat16)

    for j in range(length):
        source = line_order(z, length, j)[0] if j else z
        blocks = [2 * source + y, 2 * source + 1 - y]
        for block in blocks[0 if j else 1:]:
            twin_arrival(block)
        for block in blocks:
            attend(block)
        send_attended(source)
        if j == length - 1:
            for i in range(W_CROSS):
                w_forward(i)
        if j == 0:
            pl.when(jnp.logical_not(inner))(far_lines)
            for k in range(3, length):
                line_arrival(k, start=False)
                pair_arrival(k - 1)
            for copy in w_pairs:
                go(copy)
        if j == 1:
            pair_arrival(length - 1)

    owner_head = z // (length // 2)
    column = z % (length // 2)
    out_rows = asks // 2
    w_width = w_in.shape[1]
    crossings, returns = [], []

    def attended_arrival(j, start=True, note=True):
        source, travel = line_order(z, length, j, 1)
        lane = (1 - travel) // 2
        nxt = z + travel
        for i in range(length):
            place = line_order(source, length, i)[0] if i else source
            slot = gathered.at[source, pl.ds(2 * place, 2)]
            copy = remote(
                slot, slot, att_sem.at[0, lane, source, place], att_sem.at[1, lane, source, place],
                span=2 * ((nxt + length) % length) + y,
            )
            if start:
                copy.wait_recv()
            go(copy, (nxt >= 0) & (nxt < length), start=start, note=note)

    def project(slot, k, rows_ref, place):
        whole = jnp.concatenate([rows_ref[m] for m in range(n)], axis=1)
        value = dot(whole, w_all[k]).astype(jnp.bfloat16)
        partial[slot, k, 0] = value[:out_rows]
        partial[slot, k, 1] = value[out_rows:]
        copy = remote(
            partial.at[slot, k, other], crossed.at[slot, k], cross_sem.at[0, slot, k], cross_sem.at[1, slot, k], head=other,
        )
        go(copy)
        crossings.append((copy, slot, k, place))

    def give_back():
        copy, slot, k, place = crossings[len(returns)]
        copy.wait_recv()
        total = partial[slot, k, head].astype(jnp.float32) + crossed[slot, k].astype(jnp.float32)
        summed[slot, k] = total.astype(jnp.bfloat16)
        copy = remote(
            summed.at[slot, k], back.at[column, head, k], send_sem.at[slot, k], back_sem.at[column, head, k],
            span=2 * place + y, head=owner_head,
        )
        if slot == 0:
            @pl.when(head == owner_head)
            def _():
                back[column, head, k] = summed[slot, k]

            go(copy, head != owner_head)
        else:
            go(copy)
        returns.append(copy)

    loads[2].wait()
    loads[3].wait()
    arrived = [(att_ref, z)]

    for j in range(1, length):
        source = line_order(z, length, j, 1)[0]
        arrived.append((gathered.at[source], source))

    def last_arrival():
        attended_arrival(length - 1, note=False)

    def work(slot, k):
        project(slot, k, *arrived[slot])
        if len(crossings) > 1:
            give_back()
    work(0, y)
    for j in range(1, length - 1):
        attended_arrival(j)
        work(j, y)
    pl.when(inner)(last_arrival)
    for i in range(W_CROSS, W_CUTS - W_CROSS):
        w_pairs[i].wait_recv()
    for i in range(W_CROSS):
        w_arrival(i)
    for j in range(length - 1):
        work(j, 1 - y)
    pl.when(jnp.logical_not(inner))(last_arrival)
    attended_arrival(length - 1, start=False)
    work(length - 1, y)
    work(length - 1, 1 - y)
    give_back()

    stored = []
    for j in range(length // 2):
        for source in range(2):
            for k in range(2):
                local = (head * (length // 2) + j == z) & (head == source)

                @pl.when(jnp.logical_not(local))
                def _():
                    remote(
                        summed.at[0, 0], back.at[j, source, k], send_sem.at[0, 0], back_sem.at[j, source, k], head=other,
                    ).wait_recv()

                lanes = pl.ds((2 * j + k) * w_width, w_width)
                lines = pl.ds(source * out_rows, out_rows)
                states_ref[lines, lanes] = (
                    states_ref[lines, lanes].astype(jnp.float32) + back[j, source, k].astype(jnp.float32)
                ).astype(jnp.bfloat16)
                copy = pltpu.make_async_copy(
                    states_ref.at[lines, lanes], out_ref.at[lines, lanes], local_sem.at[11 + len(stored)],
                )
                copy.start()
                stored.append(copy)
    for copy in stored:
        copy.wait()
    for copy, cond in pending:
        if cond is None:
            copy.wait_send()
        else:
            pl.when(cond)(copy.wait_send)


def out_kernel(n, *refs):
    barrier, greeted = greet_all(n)
    pl.semaphore_wait(barrier, greeted)
    out_stage(n, *refs)


def out_stage(
    n, att_ref, w_ref, states_ref, out_ref,
    gathered, part, crossed, summed, back, ring_sem, cross_sem, send_sem, back_sem,
):
    me = lax.axis_index("span")
    head = lax.axis_index("head")
    other = 1 - head
    half = n // 2
    owner_head = me // half
    column = me % half
    rows = att_ref.shape[0]
    half_rows = rows // 2
    width = w_ref.shape[1]

    def pieces(ref):
        return [ref.at[pl.ds(k * half_rows, half_rows)] for k in range(2)]

    ring = Ring(n, pieces(att_ref), lambda block: pieces(gathered.at[block]), ring_sem)
    ring.start()
    crossings, returns = [], []

    def project(block, rows_ref):
        i = len(crossings)
        value = jnp.dot(rows_ref[...], w_ref[...], preferred_element_type=jnp.float32)
        value = value.astype(jnp.bfloat16)
        part[i, 0] = value[:half_rows]
        part[i, 1] = value[half_rows:]
        copy = remote(part.at[i, other], crossed.at[i], cross_sem.at[0, i], cross_sem.at[1, i], head=other)
        crossings.append((copy, block))

    def send_across():
        crossings[-1][0].start()

    def give_back():
        i = len(returns)
        copy, block = crossings[i]
        copy.wait_recv()
        total = part[i, head].astype(jnp.float32) + crossed[i].astype(jnp.float32)
        summed[i] = total.astype(jnp.bfloat16)
        copy = remote(
            summed.at[i], back.at[column, head], send_sem.at[i], back_sem.at[column, head],
            span=block, head=owner_head,
        )
        if i == 0:
            @pl.when(head != owner_head)
            def _():
                copy.start()

            @pl.when(head == owner_head)
            def _():
                back[column, head] = summed[i]
        else:
            copy.start()
        returns.append(copy)

    project(me, att_ref)
    send_across()
    for t in range(ring.steps):
        for block in ring.advance(t):
            project(block, gathered.at[block])
            send_across()
            give_back()
    give_back()

    for j in range(half):
        for source in range(2):
            mine = (head * half + j == me) & (head == source)

            @pl.when(jnp.logical_not(mine))
            def _():
                remote(
                    summed.at[0], back.at[j, source], send_sem.at[0], back_sem.at[j, source], head=other,
                ).wait_recv()

            lanes = pl.ds(j * width, width)
            lines = pl.ds(source * half_rows, half_rows)
            out_ref[lines, lanes] = (
                states_ref[lines, lanes].astype(jnp.float32) + back[j, source].astype(jnp.float32)
            ).astype(jnp.bfloat16)
    ring.finish()
    for copy, _ in crossings:
        copy.wait_send()
    for i, copy in enumerate(returns):
        if i == 0:
            @pl.when(head != owner_head)
            def _():
                copy.wait_send()
        else:
            copy.wait_send()


def call(kernel, collective_id, out_shape, scratch_shapes, spaces, *operands, out_space=pltpu.VMEM):
    return pl.pallas_call(
        kernel,
        out_shape=out_shape,
        in_specs=[pl.BlockSpec(memory_space=space) for space in spaces],
        out_specs=[pl.BlockSpec(memory_space=out_space)] * len(out_shape),
        scratch_shapes=scratch_shapes,
        compiler_params=pltpu.CompilerParams(collective_id=collective_id, has_side_effects=True),
    )(*operands)


def decode(encoded, kv_all, span_queries, span_count):
    dec_kv = jnp.einsum(
        "re,nsec->rsnc", encoded.reshape(-1, E), kv_all, preferred_element_type=jnp.float32
    ).astype(jnp.bfloat16)
    head_count = span_queries.shape[1] // HD
    dec_kv = dec_kv.reshape(NB, span_count, PT, 2, head_count, HD)
    dec_query = span_queries.reshape(span_count, CT, head_count, HD)
    scores = jnp.einsum(
        "cqhd,ncphd->chqnp", dec_query, dec_kv[:, :, :, 0], preferred_element_type=jnp.float32
    ) / math.sqrt(HD)
    scores = scores.reshape(span_count, head_count, CT, NB * PT)
    weights = softmax_rows(scores).astype(jnp.bfloat16)
    weights = weights.reshape(span_count, head_count, CT, NB, PT)
    attended = jnp.einsum(
        "chqnp,ncphd->cqhd", weights, dec_kv[:, :, :, 1], preferred_element_type=jnp.float32
    )
    return attended.astype(jnp.bfloat16).reshape(span_count * CT, head_count * HD)


def body(
    span_states,
    span_queries,
    span_memory,
    passages,
    neighbours,
    enc_query_w,
    enc_out_w,
    kv_weight,
    out_weight,
):
    n = lax.axis_size("span")
    span_count = neighbours.shape[0]
    bf16 = jnp.bfloat16
    dma = pltpu.SemaphoreType.DMA
    half_rows = PT // 2
    memory = span_memory.transpose(1, 2, 0)
    rows, tokens = span_count * PT, span_memory.shape[0]
    sds = jax.ShapeDtypeStruct
    states, width = sds(span_states.shape, bf16), out_weight.shape[1]
    half = tokens // 2
    operands = (neighbours, passages.reshape(-1, 2, half_rows, E), memory, enc_query_w.T, enc_out_w.T)
    pas_scratch = [pltpu.VMEM((passages.shape[0] // PT, 2, half_rows, E), bf16)]
    scratch = [
        pltpu.VMEM((8, 128), jnp.int32),
        pltpu.VMEM((n, 8, 128), jnp.int32),
        pltpu.SMEM((n, 8, 128), jnp.int32),
        pltpu.VMEM((n, half_rows, E), bf16),
        pltpu.VMEM((n, half_rows, E), bf16),
        pltpu.VMEM((span_count, half_rows, E), bf16),
        pltpu.VMEM((rows, E), bf16),
        pltpu.VMEM((2, E, tokens), bf16),
        pltpu.VMEM((E, E), bf16),
        pltpu.VMEM((E, E), bf16),
        pltpu.VMEM((rows, E), bf16),
        pltpu.VMEM((rows, E), bf16),
        dma((11 + 4 * n,)),
        dma((2, n)),
        dma((2, n)),
        dma((2, span_count)),
        dma((2, 4)),
        dma((2,)),
    ]
    if kv_weight.shape[2] == HD and n % 4 == 0:
        length = n // 2
        line_scratch = [
            pltpu.VMEM((NB, rows, E), bf16),
            pltpu.VMEM((n, E, 2 * HD), bf16),
            pltpu.VMEM((n, tokens, HD), bf16),
            pltpu.VMEM((2,) + out_weight.shape, bf16),
            pltpu.VMEM(span_states.shape, bf16),
            pltpu.VMEM((length, n, tokens, HD), bf16),
            pltpu.VMEM((length, 2, 2, half, width), bf16),
            pltpu.VMEM((length, 2, half, width), bf16),
            pltpu.VMEM((length, 2, half, width), bf16),
            pltpu.VMEM((length // 2, 2, 2, half, width), bf16),
        ]
        line_sems = [
            dma((2, length, 2, KV_CUTS)),
            dma((2, length, KV_CUTS)),
            dma((2, n, KV_CUTS)),
            dma((2, W_CUTS)),
            dma((2, W_CUTS)),
            dma((2, 2, length, length)),
            dma((2, length, 2)),
            dma((length, 2)),
            dma((length // 2, 2, 2)),
        ]
        return call(
            functools.partial(span_kernel, n, span_count), 2, [states],
            line_scratch + [pltpu.VMEM((2 * E, HD), bf16), pltpu.VMEM((2 * E, HD), jnp.float32)] + pas_scratch + [pltpu.VMEM(span_queries.shape, bf16)] + scratch + line_sems,
            [pltpu.VMEM] + [pl.ANY] * 8,
            *operands, kv_weight.reshape(2 * E, HD), span_queries, out_weight, span_states,
            out_space=pl.ANY,
        )[0]
    kv = kv_weight.transpose(1, 0, 2)
    out_scratch = [
        pltpu.VMEM((n,) + span_queries.shape, bf16),
        pltpu.VMEM((n, 2, half, width), bf16),
        pltpu.VMEM((n, half, width), bf16),
        pltpu.VMEM((n, half, width), bf16),
        pltpu.VMEM((n // 2, 2, half, width), bf16),
        dma((2, 2, n // 2, 2)),
        dma((2, n)),
        dma((n,)),
        dma((n // 2, 2)),
    ]
    found = call(
        functools.partial(fetch_kernel, n, span_count), 0,
        [sds((NB, rows, E), bf16), sds((n,) + kv.shape, bf16)],
        pas_scratch + scratch + [dma((2, 2, n // 2, 4)), dma((2, 2, n // 2, 2))], [pltpu.VMEM] + [pl.ANY] * 5,
        *operands, kv,
    )
    attended = decode(found[0], found[1], span_queries, span_count)
    return call(
        functools.partial(out_kernel, n), 1, [states], out_scratch, [pltpu.VMEM] * 3,
        attended, out_weight, span_states,
    )[0]


def solution(mesh):
    placed = (
        P(("groups", "span"), "head"),
        P(("groups", "span"), "head"),
        P(("groups", "span"), None, "head"),
        P(("groups", "span"), None),
        P(("groups", "span"), None),
        P(None, "head"),
        P(None, "head"),
        P(None, None, ("head", "span")),
        P("head", "span"),
    )
    return jax.shard_map(
        body, mesh=mesh, in_specs=placed, out_specs=P(("groups", "span"), "head"), check_vma=False
    )
```

```python
import functools
import math

import jax
import jax.numpy as jnp
from jax import lax
from jax.experimental import pallas as pl
from jax.experimental.pallas import tpu as pltpu
from jax.sharding import PartitionSpec as P

HD = 128
E = 896
EHD = 64
CT = 64
PT = 128
NB = 2
PS_DEV = 8
MESH = pl.DeviceIdType.MESH


epsilon = 1e-06


def rms_rows(values):
    return values * lax.rsqrt(jnp.mean(values * values, axis=-1, keepdims=True) + epsilon)


def softmax_rows(scores):
    top_score = jnp.max(scores, axis=-1, keepdims=True)
    raised = jnp.exp(scores - top_score)
    return raised / jnp.sum(raised, axis=-1, keepdims=True)


def ring_place(span, n):
    odd = span % 2
    return (1 - odd) * (span // 2) + odd * (n - 1 - span // 2)


def ring_span(place, n):
    back = place // (n // 2)
    return (1 - back) * (2 * place) + back * (2 * (n - 1 - place) + 1)


def remote(src, dst, send_sem, recv_sem, **where):
    return pltpu.make_async_remote_copy(
        src_ref=src, dst_ref=dst, send_sem=send_sem, recv_sem=recv_sem,
        device_id=where, device_id_type=MESH,
    )


class Ring:
    def __init__(self, n, own, slots, sems):
        me = lax.axis_index("span")
        self.n, self.own, self.slots, self.sems = n, own, slots, sems
        self.place = ring_place(me, n)
        self.targets = (ring_span((self.place + 1) % n, n), ring_span((self.place + n - 1) % n, n))
        self.steps = n // 2
        self.copies = {}

    def travels(self, t, side, k):
        return t < self.steps - 1 or k % 2 == side

    def block(self, t, side):
        n = self.n
        return ring_span((self.place + (n - t if side == 0 else t)) % n, n)

    def send(self, t, side, k):
        dst = self.slots(self.block(t, side))[k]
        copy = remote(
            self.own[k] if t == 0 else dst, dst,
            self.sems.at[0, side, t, k], self.sems.at[1, side, t, k], span=self.targets[side],
        )
        copy.start()
        self.copies[t, side, k] = copy

    def start(self):
        for k in range(len(self.own)):
            for side in range(2):
                if self.travels(0, side, k):
                    self.send(0, side, k)

    def advance(self, t, forward=None):
        for k in range(len(self.own)):
            for side in range(2):
                if self.travels(t, side, k):
                    self.copies[t, side, k].wait_recv()
                    if t + 1 < self.steps and self.travels(t + 1, side, k):
                        self.send(t + 1, side, k)
                    if forward is not None:
                        forward(t, side, k, self.block(t + 1, side))
        return [self.block(t + 1, side) for side in range(1 if t == self.steps - 1 else 2)]

    def finish(self):
        for copy in self.copies.values():
            copy.wait_send()


def weigh(scores, mask):
    scores = jnp.where(mask, scores, -jnp.inf)
    raised = jnp.exp(scores - jnp.max(scores, axis=-1, keepdims=True))
    return (raised * (1.0 / jnp.sum(raised, axis=-1, keepdims=True))).astype(jnp.bfloat16)


def same_span(shape, rows_each, lanes_each, spans):
    row = lax.broadcasted_iota(jnp.int32, shape, 0) // rows_each
    lane = (lax.broadcasted_iota(jnp.int32, shape, 1) // lanes_each) % spans
    return row == lane


def dot(a, b, dims=((1,), (0,))):
    return lax.dot_general(a, b, (dims, ((), ())), preferred_element_type=jnp.float32)


def greet_all(n):
    me = lax.axis_index("span")
    head = lax.axis_index("head")
    barrier = pltpu.get_barrier_semaphore()
    for d in range(n):
        for hop in range(2):
            if d or hop:
                pl.semaphore_signal(
                    barrier, inc=1,
                    device_id={"span": (me + d) % n, "head": (head + hop) % 2}, device_id_type=MESH,
                )
    return barrier, 2 * n - 1


def fetch_kernel(
    n, spans, nb_ref, pas_in, mem_ref, wq_ref, wo_ref, kv_ref, enc, kvg,
    pas_ref, nb_own, nbg, nbs, picks, got, swap, cop, mem, wq, wo, query, mixed,
    local_sem, nb_sem, pas_sem, swap_sem, w_sem, enc_sem, ring_sem, twin_sem,
):
    me = lax.axis_index("span")
    head = lax.axis_index("head")
    group = lax.axis_index("groups")
    other = 1 - head
    twin = group + 1 - 2 * (group % 2)
    part = group % 2
    half_rows = PT // 2
    half_e = wq_ref.shape[0]
    barrier, greeted = greet_all(n)
    pl.semaphore_signal(barrier, inc=1, device_id={"groups": twin}, device_id_type=MESH)
    loads = [pltpu.make_async_copy(pas_in, pas_ref, local_sem.at[7])]
    for copy in loads:
        copy.start()
    nb_own[...] = jnp.zeros_like(nb_own)
    nb_own[:spans, :NB] = nb_ref[...]
    pl.semaphore_wait(barrier, greeted + 1)

    nb_copies = []
    for d in range(1, n):
        copy = remote(nb_own, nbg.at[me], nb_sem.at[0, d], nb_sem.at[1, d], span=(me + d) % n)
        copy.start()
        nb_copies.append(copy)
    own_nb = pltpu.make_async_copy(nb_own, nbg.at[me], local_sem.at[0])
    own_nb.start()

    depth = kv_ref.shape[1]
    half, extra = depth // 2, depth // 28 * 3
    near, far = part, 1 - part

    def pieces(ref):
        return [
            ref.at[near, pl.ds(0, half)], ref.at[near, pl.ds(half, half)],
            ref.at[far, pl.ds(0, extra // 2)], ref.at[far, pl.ds(extra // 2, extra // 2)],
        ]

    ring = Ring(n, pieces(kv_ref), lambda block: pieces(kvg.at[block]), ring_sem)
    twins = [[] for _ in range(ring.steps)]

    def to_twin(t, side, k, block):
        if k < 2:
            lines = pl.ds(extra, half - extra) if k == 0 else pl.ds(half, half)
            piece = kvg.at[block, near, lines]
            copy = remote(piece, piece, twin_sem.at[0, side, t, k], twin_sem.at[1, side, t, k], groups=twin)
            copy.start()
            twins[t].append(copy)

    ring.start()
    mine = pl.ds(pl.multiple_of(head * half_e, half_e), half_e)
    w_copies, own_copies = [], []
    for i, (src, dst) in enumerate((
        (mem_ref.at[0], mem.at[0, mine]), (mem_ref.at[1], mem.at[1, mine]), (wq_ref, wq.at[mine]), (wo_ref, wo.at[mine]),
    )):
        w_copies.append(remote(src, dst, w_sem.at[0, i], w_sem.at[1, i], head=other))
        w_copies[-1].start()
        own_copies.append(pltpu.make_async_copy(src, dst, local_sem.at[3 + i]))
        own_copies[-1].start()
    own_copies.append(pltpu.make_async_copy(kv_ref, kvg.at[me], local_sem.at[1]))
    own_copies[-1].start()
    own_nb.wait()
    loads[0].wait()
    for copy in nb_copies:
        copy.wait()
    to_scalar = pltpu.make_async_copy(nbg, nbs, local_sem.at[2])
    to_scalar.start()
    to_scalar.wait()

    def pick(requester):
        index = jnp.int32(0)
        for e in range(spans * NB):
            wanted = nbs[requester, e // NB, e % NB]
            index = index + jnp.where(wanted // PS_DEV == me, wanted % PS_DEV, 0)
        return pas_ref[index, head]

    pas_copies = []
    picks[1] = pick((me + 1) % n)
    for d in range(1, n):
        if d + 1 < n:
            picks[d + 1] = pick((me + d + 1) % n)
        else:
            got[me] = pick(me)
        copy = remote(picks.at[d], got.at[me], pas_sem.at[0, d], pas_sem.at[1, d], span=(me + d) % n)
        copy.start()
        pas_copies.append(copy)

    arrivals = [ring.advance(0, to_twin)]
    for copy in pas_copies:
        copy.wait_recv()
    swaps = []
    for c in range(spans):
        swap[c] = got[nbs[me, c, other] // PS_DEV]
    for c in range(spans):
        spot = cop.at[pl.ds(pl.multiple_of(c * PT + head * half_rows, half_rows), half_rows)]
        copy = remote(swap.at[c], spot, swap_sem.at[0, c], swap_sem.at[1, c], head=other)
        copy.start()
        swaps.append(copy)
        spot[...] = got[nbs[me, c, head] // PS_DEV]
    for copy in own_copies:
        copy.wait()
    for copy in w_copies:
        copy.wait()
    for copy in swaps:
        copy.wait()

    arrivals.append(ring.advance(1, to_twin))
    rows = cop.shape[0]
    tokens = mem.shape[2]
    width = cop.shape[1]
    values = cop[...].astype(jnp.float32)
    query[...] = dot(rms_rows(values).astype(jnp.bfloat16), wq[...], ((1,), (1,))).astype(jnp.bfloat16)
    mask = same_span((rows, tokens), PT, CT, spans)
    feature = lax.broadcasted_iota(jnp.int32, (2 * EHD, tokens), 0) // EHD
    for j in range(width // (2 * EHD)):
        lines = pl.ds(j * 2 * EHD, 2 * EHD)
        total = None
        for e in range(2):
            keys = jnp.where(feature == e, mem[0, lines], jnp.bfloat16(0))
            vals = jnp.where(feature == e, mem[1, lines], jnp.bfloat16(0))
            scores = dot(query[:, lines], keys) * (1.0 / math.sqrt(EHD))
            term = dot(weigh(scores, mask), vals, ((1,), (1,)))
            total = term if e == 0 else total + term
        mixed[:, lines] = total.astype(jnp.bfloat16)
    branch = dot(mixed[...], wo[...])
    enc[head] = rms_rows(cop[...].astype(jnp.float32) + branch).astype(jnp.bfloat16)
    enc_copy = remote(enc.at[head], enc.at[head], enc_sem.at[0], enc_sem.at[1], head=other)
    enc_copy.start()
    if ring.steps > 2:
        arrivals.append(ring.advance(2, to_twin))
    enc_copy.wait_recv()

    for t in range(ring.steps):
        while len(arrivals) < min(t + 3, ring.steps):
            arrivals.append(ring.advance(len(arrivals), to_twin))
        for copy in twins[t]:
            copy.wait_recv()
    enc_copy.wait_send()
    for copy in pas_copies + [copy for pair in twins for copy in pair]:
        copy.wait_send()
    ring.finish()


W_CUTS = 4
W_CROSS = 1
KV_EXTRA = 6
KV_CUTS = 2


def line_order(z, length, j, first=-1):
    far_half = z // max(1, length // 2)
    short = (1 - far_half) * z + far_half * (length - 1 - z)
    way = 1 - 2 * far_half
    both = (2 * short - j + 2 * length) // (2 * length)
    turn = first * (2 * (j % 2) - 1)
    source = z + both * turn * way * ((j + 1) // 2) + (1 - both) * way * (j - short)
    travel = -(both * turn * way + (1 - both) * way)
    return source, travel


def span_kernel(
    n, spans, nb_ref, pas_in, mem_ref, wq_ref, wo_ref, kv_ref, ask_in, w_in, states_in, out_ref,
    enc, kvg, att_ref, w_all, states_ref, gathered, partial, crossed, summed, back,
    kv_rows, kv_wide, pas_ref, ask_ref, nb_own, nbg, nbs, picks, got, swap, cop, mem, wq, wo, query, mixed,
    local_sem, nb_sem, pas_sem, swap_sem, w_sem, enc_sem, kvz_sem, kvy_sem, kvx_sem,
    wy_sem, wx_sem, att_sem, cross_sem, send_sem, back_sem,
):
    me = lax.axis_index("span")
    head = lax.axis_index("head")
    group = lax.axis_index("groups")
    other = 1 - head
    twin = group + 1 - 2 * (group % 2)
    plane = group % 2
    length = n // 2
    z, y = me // 2, me % 2
    half_rows = PT // 2
    half_e = wq_ref.shape[0]
    pending = []

    def go(copy, cond=None, start=True, note=True):
        if start:
            if cond is None:
                copy.start()
            else:
                pl.when(cond)(copy.start)
        if note:
            pending.append((copy, cond))

    barrier, greeted = greet_all(n)
    pl.semaphore_signal(barrier, inc=1, device_id={"groups": twin}, device_id_type=MESH)
    depth = kv_ref.shape[0] // 2
    kv_load = pltpu.make_async_copy(kv_ref, kv_rows, local_sem.at[1])
    kv_load.start()
    loads = [
        pltpu.make_async_copy(pas_in, pas_ref, local_sem.at[7]),
        pltpu.make_async_copy(ask_in, ask_ref, local_sem.at[8]),
        pltpu.make_async_copy(w_in, w_all.at[y], local_sem.at[9]),
        pltpu.make_async_copy(states_in, states_ref, local_sem.at[10]),
    ]
    for copy in loads:
        copy.start()
    nb_own[...] = jnp.zeros_like(nb_own)
    nb_own[:spans, :NB] = nb_ref[...]
    kv_load.wait()
    kv_wide[...] = kv_rows[...].astype(jnp.float32)
    for i in range(2):
        kvg[me, :, pl.ds(i * HD, HD)] = kv_wide[pl.ds(i, depth, stride=2)].astype(jnp.bfloat16)
    pl.semaphore_wait(barrier, greeted + 1)

    for d in range(1, n):
        go(remote(nb_own, nbg.at[me], nb_sem.at[0, d], nb_sem.at[1, d], span=(me + d) % n))
    own_nb = pltpu.make_async_copy(nb_own, nbg.at[me], local_sem.at[0])
    own_nb.start()

    half, extra = depth // 2, depth // 56 * KV_EXTRA
    cut = (half + extra) // KV_CUTS
    parts = range(KV_CUTS)

    def from_edge(side, offset, size):
        return pl.ds(pl.multiple_of((1 - side) * offset + side * (depth - offset - size), 16), size)

    def plane_part(i):
        return from_edge(plane, i * cut, cut)

    def cross_part(side, i):
        start = min(i * cut, half - extra)
        return from_edge(side, start, min((i + 1) * cut, half - extra) - start)

    crossed_parts = [i for i in parts if i * cut < half - extra]

    def along(source, travel, i, **how):
        lines = plane_part(i)
        spot = kvg.at[2 * source + y, lines]
        nxt = z + travel
        lane = (1 - travel) // 2
        copy = remote(
            spot, spot, kvz_sem.at[0, source, lane, i], kvz_sem.at[1, source, lane, i],
            span=2 * ((nxt + length) % length) + y,
        )
        go(copy, (nxt >= 0) & (nxt < length), **how)

    def to_pair(source, i, **how):
        lines = plane_part(i)
        spot = kvg.at[2 * source + y, lines]
        go(remote(
            spot, spot, kvy_sem.at[0, source, i], kvy_sem.at[1, source, i],
            span=2 * z + 1 - y,
        ), **how)

    def to_twin(block, i, **how):
        if i in crossed_parts:
            spot = kvg.at[block, cross_part(plane, i)]
            go(remote(spot, spot, kvx_sem.at[0, block, i], kvx_sem.at[1, block, i], groups=twin), **how)

    def line_arrival(j, start=True, note=True):
        source, travel = line_order(z, length, j)
        lane = (1 - travel) // 2
        block = 2 * source + y
        for i in parts:
            spot = kvg.at[block, plane_part(i)]
            if start:
                remote(
                    spot, spot, kvz_sem.at[0, source, lane, i], kvz_sem.at[1, source, lane, i], span=2 * z + 1 - y,
                ).wait_recv()
            along(source, travel, i, start=start, note=note)
            to_pair(source, i, start=start, note=note)
            to_twin(block, i, start=start, note=note)

    def pair_arrival(j):
        source = z if j == 0 else line_order(z, length, j)[0]
        block = 2 * source + 1 - y
        for i in parts:
            spot = kvg.at[block, plane_part(i)]
            remote(spot, spot, kvy_sem.at[0, source, i], kvy_sem.at[1, source, i], span=2 * z + 1 - y).wait_recv()
            to_twin(block, i)

    def twin_arrival(block):
        for i in crossed_parts:
            spot = kvg.at[block, cross_part(1 - plane, i)]
            remote(spot, spot, kvx_sem.at[0, block, i], kvx_sem.at[1, block, i], groups=twin).wait_recv()

    for i in parts:
        for travel in (1, -1):
            along(z, travel, i)
        to_pair(z, i)

    mine = pl.ds(pl.multiple_of(head * half_e, half_e), half_e)
    w_copies, own_copies = [], []
    for i, (src, dst) in enumerate((
        (mem_ref.at[0], mem.at[0, mine]), (mem_ref.at[1], mem.at[1, mine]), (wq_ref, wq.at[mine]), (wo_ref, wo.at[mine]),
    )):
        w_copies.append(remote(src, dst, w_sem.at[0, i], w_sem.at[1, i], head=other))
        w_copies[-1].start()
        own_copies.append(pltpu.make_async_copy(src, dst, local_sem.at[3 + i]))
        own_copies[-1].start()
    own_nb.wait()
    loads[0].wait()
    for d in range(1, n):
        pending[d - 1][0].wait_recv()
    to_scalar = pltpu.make_async_copy(nbg, nbs, local_sem.at[2])
    to_scalar.start()
    to_scalar.wait()

    def pick(requester):
        index = jnp.int32(0)
        for e in range(spans * NB):
            wanted = nbs[requester, e // NB, e % NB]
            index = index + jnp.where(wanted // PS_DEV == me, wanted % PS_DEV, 0)
        return pas_ref[index, head]

    pas_copies = []
    picks[1] = pick((me + 1) % n)
    for d in range(1, n):
        if d + 1 < n:
            picks[d + 1] = pick((me + d + 1) % n)
        else:
            got[me] = pick(me)
        copy = remote(picks.at[d], got.at[me], pas_sem.at[0, d], pas_sem.at[1, d], span=(me + d) % n)
        go(copy)
        pas_copies.append(copy)
    line_arrival(1)
    pair_arrival(0)
    inner = (z > 0) & (z < length - 1)
    pl.when(inner)(lambda: line_arrival(2, note=False))
    for copy in pas_copies:
        copy.wait_recv()
    swaps = []
    for c in range(spans):
        swap[c] = got[nbs[me, c, other] // PS_DEV]
    for c in range(spans):
        spot = cop.at[pl.ds(pl.multiple_of(c * PT + head * half_rows, half_rows), half_rows)]
        copy = remote(swap.at[c], spot, swap_sem.at[0, c], swap_sem.at[1, c], head=other)
        copy.start()
        swaps.append(copy)
        spot[...] = got[nbs[me, c, head] // PS_DEV]
    pl.when(jnp.logical_not(inner))(lambda: line_arrival(2, note=False))
    line_arrival(2, start=False)
    pair_arrival(1)
    for copy in own_copies:
        copy.wait()
    for copy in w_copies:
        copy.wait()
    for copy in swaps:
        copy.wait()
    rows = cop.shape[0]
    tokens = mem.shape[2]
    width = cop.shape[1]
    values = cop[...].astype(jnp.float32)
    query[...] = dot(rms_rows(values).astype(jnp.bfloat16), wq[...], ((1,), (1,))).astype(jnp.bfloat16)
    mask = same_span((rows, tokens), PT, CT, spans)
    feature = lax.broadcasted_iota(jnp.int32, (2 * EHD, tokens), 0) // EHD
    for j in range(width // (2 * EHD)):
        lines = pl.ds(j * 2 * EHD, 2 * EHD)
        total = None
        for e in range(2):
            keys = jnp.where(feature == e, mem[0, lines], jnp.bfloat16(0))
            vals = jnp.where(feature == e, mem[1, lines], jnp.bfloat16(0))
            scores = dot(query[:, lines], keys) * (1.0 / math.sqrt(EHD))
            term = dot(weigh(scores, mask), vals, ((1,), (1,)))
            total = term if e == 0 else total + term
        mixed[:, lines] = total.astype(jnp.bfloat16)
    branch = dot(mixed[...], wo[...])
    enc[head] = rms_rows(cop[...].astype(jnp.float32) + branch).astype(jnp.bfloat16)
    enc_copy = remote(enc.at[head], enc.at[head], enc_sem.at[0], enc_sem.at[1], head=other)
    go(enc_copy)
    w_chunk = w_in.shape[0] // W_CUTS

    def w_part(side, i):
        lines = (1 - side) * i + side * (W_CUTS - 1 - i)
        return pl.ds(pl.multiple_of(lines * w_chunk, 16), w_chunk)

    w_pairs = []
    for i in range(W_CUTS - W_CROSS):
        lines = w_part(plane, i)
        w_pairs.append(remote(
            w_in.at[lines], w_all.at[y, lines], wy_sem.at[0, i], wy_sem.at[1, i], span=2 * z + 1 - y,
        ))

    def w_forward(i):
        w_pairs[i].wait_recv()
        spot = w_all.at[1 - y, w_part(plane, i)]
        go(remote(spot, spot, wx_sem.at[0, i], wx_sem.at[1, i], groups=twin))

    def w_arrival(i):
        spot = w_all.at[1 - y, w_part(1 - plane, i)]
        remote(spot, spot, wx_sem.at[0, i], wx_sem.at[1, i], groups=twin).wait_recv()

    def far_lines():
        for k in range(3, length):
            line_arrival(k, note=False)
    pl.when(inner)(far_lines)
    enc_copy.wait_recv()

    loads[1].wait()
    asks = ask_ref.shape[0]
    def send_attended(place):
        spot = pl.ds(2 * place, 2)
        for travel in (1, -1):
            nxt = z + travel
            lane = (1 - travel) // 2
            copy = remote(
                att_ref.at[spot], gathered.at[z, spot], att_sem.at[0, lane, z, place], att_sem.at[1, lane, z, place],
                span=2 * ((nxt + length) % length) + y,
            )
            go(copy, (nxt >= 0) & (nxt < length))

    dec_mask = same_span((asks, NB * rows), CT, PT, spans)

    def attend(block):
        flat = enc[...].reshape(NB * rows, width)
        keys = dot(flat, kvg[block, :, pl.ds(0, HD)]).astype(jnp.bfloat16)
        vals = dot(flat, kvg[block, :, pl.ds(HD, HD)]).astype(jnp.bfloat16)
        spot = pl.ds(pl.multiple_of(block * HD, HD), HD)
        scores = dot(ask_ref[:, spot], keys, ((1,), (1,))) * (1.0 / math.sqrt(HD))
        att_ref[block] = dot(weigh(scores, dec_mask), vals).astype(jnp.bfloat16)

    for j in range(length):
        source = line_order(z, length, j)[0] if j else z
        blocks = [2 * source + y, 2 * source + 1 - y]
        for k, block in enumerate(blocks):
            if j or k:
                twin_arrival(block)
            if j == length - 1:
                attend(block)
        if j < length - 1:
            for block in blocks:
                attend(block)
        send_attended(source)
        if j == length - 1:
            for i in range(W_CROSS):
                w_forward(i)
        if j == 0:
            pl.when(jnp.logical_not(inner))(far_lines)
            for k in range(3, length):
                line_arrival(k, start=False)
                pair_arrival(k - 1)
            for copy in w_pairs:
                go(copy)
        if j == 1:
            pair_arrival(length - 1)

    owner_head = z // (length // 2)
    column = z % (length // 2)
    out_rows = asks // 2
    w_width = w_in.shape[1]
    crossings, returns = [], []

    def attended_arrival(j, start=True, note=True):
        source, travel = line_order(z, length, j, 1)
        lane = (1 - travel) // 2
        nxt = z + travel
        for i in range(length):
            place = line_order(source, length, i)[0] if i else source
            slot = gathered.at[source, pl.ds(2 * place, 2)]
            copy = remote(
                slot, slot, att_sem.at[0, lane, source, place], att_sem.at[1, lane, source, place],
                span=2 * ((nxt + length) % length) + y,
            )
            if start:
                copy.wait_recv()
            go(copy, (nxt >= 0) & (nxt < length), start=start, note=note)

    def project(slot, k, rows_ref, place):
        whole = jnp.concatenate([rows_ref[m] for m in range(n)], axis=1)
        value = dot(whole, w_all[k]).astype(jnp.bfloat16)
        partial[slot, k, 0] = value[:out_rows]
        partial[slot, k, 1] = value[out_rows:]
        copy = remote(
            partial.at[slot, k, other], crossed.at[slot, k], cross_sem.at[0, slot, k], cross_sem.at[1, slot, k], head=other,
        )
        go(copy)
        crossings.append((copy, slot, k, place))

    def give_back():
        copy, slot, k, place = crossings[len(returns)]
        copy.wait_recv()
        total = partial[slot, k, head].astype(jnp.float32) + crossed[slot, k].astype(jnp.float32)
        summed[slot, k] = total.astype(jnp.bfloat16)
        copy = remote(
            summed.at[slot, k], back.at[column, head, k], send_sem.at[slot, k], back_sem.at[column, head, k],
            span=2 * place + y, head=owner_head,
        )
        if slot == 0:
            @pl.when(head == owner_head)
            def _():
                back[column, head, k] = summed[slot, k]

            go(copy, head != owner_head)
        else:
            go(copy)
        returns.append(copy)

    loads[2].wait()
    loads[3].wait()
    arrived = [(att_ref, z)]

    for j in range(1, length):
        source = line_order(z, length, j, 1)[0]
        arrived.append((gathered.at[source], source))

    def last_arrival():
        attended_arrival(length - 1, note=False)

    def work(slot, k):
        project(slot, k, *arrived[slot])
        if len(crossings) > 1:
            give_back()
    work(0, y)
    for j in range(1, length - 1):
        attended_arrival(j)
        work(j, y)
    pl.when(inner)(last_arrival)
    for i in range(W_CROSS, W_CUTS - W_CROSS):
        w_pairs[i].wait_recv()
    for i in range(W_CROSS):
        w_arrival(i)
    for j in range(length - 1):
        work(j, 1 - y)
    pl.when(jnp.logical_not(inner))(last_arrival)
    attended_arrival(length - 1, start=False)
    work(length - 1, y)
    work(length - 1, 1 - y)
    give_back()

    stored = []
    for j in range(length // 2):
        for source in range(2):
            for k in range(2):
                local = (head * (length // 2) + j == z) & (head == source)

                @pl.when(jnp.logical_not(local))
                def _():
                    remote(
                        summed.at[0, 0], back.at[j, source, k], send_sem.at[0, 0], back_sem.at[j, source, k], head=other,
                    ).wait_recv()

                lanes = pl.ds((2 * j + k) * w_width, w_width)
                lines = pl.ds(source * out_rows, out_rows)
                states_ref[lines, lanes] = (
                    states_ref[lines, lanes].astype(jnp.float32) + back[j, source, k].astype(jnp.float32)
                ).astype(jnp.bfloat16)
                copy = pltpu.make_async_copy(
                    states_ref.at[lines, lanes], out_ref.at[lines, lanes], local_sem.at[11 + len(stored)],
                )
                copy.start()
                stored.append(copy)
    for copy in stored:
        copy.wait()
    for copy, cond in pending:
        if cond is None:
            copy.wait_send()
        else:
            pl.when(cond)(copy.wait_send)


def out_kernel(n, *refs):
    barrier, greeted = greet_all(n)
    pl.semaphore_wait(barrier, greeted)
    out_stage(n, *refs)


def out_stage(
    n, att_ref, w_ref, states_ref, out_ref,
    gathered, part, crossed, summed, back, ring_sem, cross_sem, send_sem, back_sem,
):
    me = lax.axis_index("span")
    head = lax.axis_index("head")
    other = 1 - head
    half = n // 2
    owner_head = me // half
    column = me % half
    rows = att_ref.shape[0]
    half_rows = rows // 2
    width = w_ref.shape[1]

    def pieces(ref):
        return [ref.at[pl.ds(k * half_rows, half_rows)] for k in range(2)]

    ring = Ring(n, pieces(att_ref), lambda block: pieces(gathered.at[block]), ring_sem)
    ring.start()
    crossings, returns = [], []

    def project(block, rows_ref):
        i = len(crossings)
        value = jnp.dot(rows_ref[...], w_ref[...], preferred_element_type=jnp.float32)
        value = value.astype(jnp.bfloat16)
        part[i, 0] = value[:half_rows]
        part[i, 1] = value[half_rows:]
        copy = remote(part.at[i, other], crossed.at[i], cross_sem.at[0, i], cross_sem.at[1, i], head=other)
        crossings.append((copy, block))

    def send_across():
        crossings[-1][0].start()

    def give_back():
        i = len(returns)
        copy, block = crossings[i]
        copy.wait_recv()
        total = part[i, head].astype(jnp.float32) + crossed[i].astype(jnp.float32)
        summed[i] = total.astype(jnp.bfloat16)
        copy = remote(
            summed.at[i], back.at[column, head], send_sem.at[i], back_sem.at[column, head],
            span=block, head=owner_head,
        )
        if i == 0:
            @pl.when(head != owner_head)
            def _():
                copy.start()

            @pl.when(head == owner_head)
            def _():
                back[column, head] = summed[i]
        else:
            copy.start()
        returns.append(copy)

    project(me, att_ref)
    send_across()
    for t in range(ring.steps):
        for block in ring.advance(t):
            project(block, gathered.at[block])
            send_across()
            give_back()
    give_back()

    for j in range(half):
        for source in range(2):
            mine = (head * half + j == me) & (head == source)

            @pl.when(jnp.logical_not(mine))
            def _():
                remote(
                    summed.at[0], back.at[j, source], send_sem.at[0], back_sem.at[j, source], head=other,
                ).wait_recv()

            lanes = pl.ds(j * width, width)
            lines = pl.ds(source * half_rows, half_rows)
            out_ref[lines, lanes] = (
                states_ref[lines, lanes].astype(jnp.float32) + back[j, source].astype(jnp.float32)
            ).astype(jnp.bfloat16)
    ring.finish()
    for copy, _ in crossings:
        copy.wait_send()
    for i, copy in enumerate(returns):
        if i == 0:
            @pl.when(head != owner_head)
            def _():
                copy.wait_send()
        else:
            copy.wait_send()


def call(kernel, collective_id, out_shape, scratch_shapes, spaces, *operands, out_space=pltpu.VMEM):
    return pl.pallas_call(
        kernel,
        out_shape=out_shape,
        in_specs=[pl.BlockSpec(memory_space=space) for space in spaces],
        out_specs=[pl.BlockSpec(memory_space=out_space)] * len(out_shape),
        scratch_shapes=scratch_shapes,
        compiler_params=pltpu.CompilerParams(collective_id=collective_id, has_side_effects=True),
    )(*operands)


def decode(encoded, kv_all, span_queries, span_count):
    dec_kv = jnp.einsum(
        "re,nsec->rsnc", encoded.reshape(-1, E), kv_all, preferred_element_type=jnp.float32
    ).astype(jnp.bfloat16)
    head_count = span_queries.shape[1] // HD
    dec_kv = dec_kv.reshape(NB, span_count, PT, 2, head_count, HD)
    dec_query = span_queries.reshape(span_count, CT, head_count, HD)
    scores = jnp.einsum(
        "cqhd,ncphd->chqnp", dec_query, dec_kv[:, :, :, 0], preferred_element_type=jnp.float32
    ) / math.sqrt(HD)
    scores = scores.reshape(span_count, head_count, CT, NB * PT)
    weights = softmax_rows(scores).astype(jnp.bfloat16)
    weights = weights.reshape(span_count, head_count, CT, NB, PT)
    attended = jnp.einsum(
        "chqnp,ncphd->cqhd", weights, dec_kv[:, :, :, 1], preferred_element_type=jnp.float32
    )
    return attended.astype(jnp.bfloat16).reshape(span_count * CT, head_count * HD)


def body(
    span_states,
    span_queries,
    span_memory,
    passages,
    neighbours,
    enc_query_w,
    enc_out_w,
    kv_weight,
    out_weight,
):
    n = lax.axis_size("span")
    span_count = neighbours.shape[0]
    bf16 = jnp.bfloat16
    dma = pltpu.SemaphoreType.DMA
    half_rows = PT // 2
    memory = span_memory.transpose(1, 2, 0)
    rows, tokens = span_count * PT, span_memory.shape[0]
    sds = jax.ShapeDtypeStruct
    states, width = sds(span_states.shape, bf16), out_weight.shape[1]
    half = tokens // 2
    operands = (neighbours, passages.reshape(-1, 2, half_rows, E), memory, enc_query_w.T, enc_out_w.T)
    pas_scratch = [pltpu.VMEM((passages.shape[0] // PT, 2, half_rows, E), bf16)]
    scratch = [
        pltpu.VMEM((8, 128), jnp.int32),
        pltpu.VMEM((n, 8, 128), jnp.int32),
        pltpu.SMEM((n, 8, 128), jnp.int32),
        pltpu.VMEM((n, half_rows, E), bf16),
        pltpu.VMEM((n, half_rows, E), bf16),
        pltpu.VMEM((span_count, half_rows, E), bf16),
        pltpu.VMEM((rows, E), bf16),
        pltpu.VMEM((2, E, tokens), bf16),
        pltpu.VMEM((E, E), bf16),
        pltpu.VMEM((E, E), bf16),
        pltpu.VMEM((rows, E), bf16),
        pltpu.VMEM((rows, E), bf16),
        dma((11 + 4 * n,)),
        dma((2, n)),
        dma((2, n)),
        dma((2, span_count)),
        dma((2, 4)),
        dma((2,)),
    ]
    if kv_weight.shape[2] == HD and n % 4 == 0:
        length = n // 2
        line_scratch = [
            pltpu.VMEM((NB, rows, E), bf16),
            pltpu.VMEM((n, E, 2 * HD), bf16),
            pltpu.VMEM((n, tokens, HD), bf16),
            pltpu.VMEM((2,) + out_weight.shape, bf16),
            pltpu.VMEM(span_states.shape, bf16),
            pltpu.VMEM((length, n, tokens, HD), bf16),
            pltpu.VMEM((length, 2, 2, half, width), bf16),
            pltpu.VMEM((length, 2, half, width), bf16),
            pltpu.VMEM((length, 2, half, width), bf16),
            pltpu.VMEM((length // 2, 2, 2, half, width), bf16),
        ]
        line_sems = [
            dma((2, length, 2, KV_CUTS)),
            dma((2, length, KV_CUTS)),
            dma((2, n, KV_CUTS)),
            dma((2, W_CUTS)),
            dma((2, W_CUTS)),
            dma((2, 2, length, length)),
            dma((2, length, 2)),
            dma((length, 2)),
            dma((length // 2, 2, 2)),
        ]
        return call(
            functools.partial(span_kernel, n, span_count), 2, [states],
            line_scratch + [pltpu.VMEM((2 * E, HD), bf16), pltpu.VMEM((2 * E, HD), jnp.float32)] + pas_scratch + [pltpu.VMEM(span_queries.shape, bf16)] + scratch + line_sems,
            [pltpu.VMEM] + [pl.ANY] * 8,
            *operands, kv_weight.reshape(2 * E, HD), span_queries, out_weight, span_states,
            out_space=pl.ANY,
        )[0]
    kv = kv_weight.transpose(1, 0, 2)
    out_scratch = [
        pltpu.VMEM((n,) + span_queries.shape, bf16),
        pltpu.VMEM((n, 2, half, width), bf16),
        pltpu.VMEM((n, half, width), bf16),
        pltpu.VMEM((n, half, width), bf16),
        pltpu.VMEM((n // 2, 2, half, width), bf16),
        dma((2, 2, n // 2, 2)),
        dma((2, n)),
        dma((n,)),
        dma((n // 2, 2)),
    ]
    found = call(
        functools.partial(fetch_kernel, n, span_count), 0,
        [sds((NB, rows, E), bf16), sds((n,) + kv.shape, bf16)],
        pas_scratch + scratch + [dma((2, 2, n // 2, 4)), dma((2, 2, n // 2, 2))], [pltpu.VMEM] + [pl.ANY] * 5,
        *operands, kv,
    )
    attended = decode(found[0], found[1], span_queries, span_count)
    return call(
        functools.partial(out_kernel, n), 1, [states], out_scratch, [pltpu.VMEM] * 3,
        attended, out_weight, span_states,
    )[0]


def solution(mesh):
    placed = (
        P(("groups", "span"), "head"),
        P(("groups", "span"), "head"),
        P(("groups", "span"), None, "head"),
        P(("groups", "span"), None),
        P(("groups", "span"), None),
        P(None, "head"),
        P(None, "head"),
        P(None, None, ("head", "span")),
        P("head", "span"),
    )
    return jax.shard_map(
        body, mesh=mesh, in_specs=placed, out_specs=P(("groups", "span"), "head"), check_vma=False
    )
```
